32 devices in a mesh: dp: 16 (over z, x, core), mp: 2 (over y).
Axes of the slice: x: 2, y: 2, z: 4, core: 2. Of those that a mesh axis runs over, the one named last changes fastest.
Arguments:
- frames_in: float32 [12288, 768], P(('dp', 'mp')), may hold values from -6 to 6
- frames_cot: float32 [12288, 768], P(('dp', 'mp')), may hold values from -6 to 6
- clip_ids: int32 [12288], replicated, may hold values from 0 to 16, never falling along the last dimension, each value on 1 to 768 neighbouring positions
- frame_mask: int32 [12288], replicated, may hold values 0 or 1
- norm_gain: float32 [2, 2, 768], replicated, may hold values from 0.25 to 1.75
- norm_bias: float32 [2, 2, 768], replicated, may hold values from -2 to 2
- qkv_weight: bfloat16 [2, 768, 3, 768], P(None, 'dp', None, 'mp'), as said below
- qv_bias: float32 [2, 2, 768], P(None, None, 'mp'), may hold values from -0.4 to 0.4
- proj_weight: bfloat16 [2, 768, 768], P(None, ('mp', 'dp')), may hold values from -4 to 4
- up_weight: bfloat16 [2, 768, 3072], P(None, 'dp', 'mp'), may hold values from -0.21875 to 0.21875
- up_bias: float32 [2, 3072], P(None, 'mp'), may hold values from -3 to 3
- down_weight: bfloat16 [2, 3072, 768], P(None, ('mp', 'dp')), may hold values from -0.109375 to 0.109375
- out_biases: float32 [2, 2, 768], replicated, may hold values from -2 to 2
Outputs:
- frames_out: float32 [12288, 768], P(('dp', 'mp'))
- frames_grad: float32 [12288, 768], P(('dp', 'mp'))
- grad_qkv: float32 [2, 768, 3, 768], P(None, 'dp', None, 'mp')
- grad_qv_bias: float32 [2, 2, 768], P(None, None, 'mp')
- grad_proj: float32 [2, 768, 768], P(None, ('mp', 'dp'))
- grad_up: float32 [2, 768, 3072], P(None, 'dp', 'mp')
- grad_up_bias: float32 [2, 3072], P(None, 'mp')
- grad_down: float32 [2, 3072, 768], P(None, ('mp', 'dp'))
- grad_gain: float32 [2, 2, 768], replicated
- grad_norm_bias: float32 [2, 2, 768], replicated
- grad_out_biases: float32 [2, 2, 768], replicated
The draws below stay inside these ranges and needn't reach their ends.
Inputs may be any that keep to these rules, and one draw needn't show every extreme that they name: `clip_ids`: clip numbers never fall from one frame to the next; each clip holds 1 to 768 frames and one holds exactly 768. `qkv_weight`: projection weights for queries, keys and values.
All inputs are finite; a program needn't handle non-finite values.
Results may differ from the reference program's by a relative error of at most 0.013.
Values may be sent and summed in bfloat16 or wider, within the bound.
A program may use at most 320 MiB of HBM per device.

```python
import math
import jax
import jax.numpy as jnp
import numpy as np
from jax import lax

D = 768
H = 12
HD = 64
FF = 3072
LAYERS = 2
TOK_DEV = 768
TOKENS = 12288
CLIPS = 17


def draw_qkv_weight(key, part):
    base = jax.random.normal(key, (LAYERS, D, 3, D), jnp.float32) * D ** (-0.5)
    return base.astype(jnp.bfloat16)


def place_ends(drawn, rng, smallest, high):
    longest = drawn.shape.index(max(drawn.shape))
    spots = []
    for shift in (0, 1):
        where = [jax.random.randint(jax.random.fold_in(rng, axis), (), 0, length) for axis, length in enumerate(drawn.shape)]
        where[longest] = (where[longest] + shift) % drawn.shape[longest]
        spots.append(tuple(where))
    return drawn.at[spots[0]].set(smallest).at[spots[1]].set(high)


def shard_levels(rng, shape, split, least, high):
    factor_of = 1.0
    for dim, shards_of in split:
        steps = jax.random.uniform(jax.random.fold_in(jax.random.fold_in(rng, 6), dim), (shards_of,), jnp.float32, least / len(split), high / len(split))
        factor_of = factor_of * jnp.repeat(jnp.exp(steps), shape[dim] // shards_of).reshape((-1,) + (1,) * (len(shape) - 1 - dim))
    return factor_of


def split_up(count, total, bound, skew):
    weights = [(1 << 20) // math.isqrt(standing ** skew) + 1 for standing in range(2, count + 1)]
    rest, given = total - bound - (count - 1), [1] * (count - 1)
    while rest > 0:
        free = [i for i in range(count - 1) if given[i] < bound]
        pool, budget = sum([weights[i] for i in free]), rest
        for i in free:
            addition = min(bound - given[i], max(1, budget * weights[i] // pool), rest)
            given[i] = given[i] + addition
            rest = rest - addition
    return np.array([bound] + given)


def ragged(own_key, count, total, most, slope):
    if count == 2:
        one = jax.random.randint(own_key, (), max(1, total - most), min(most, total - 1) + 1)
        return jnp.stack([one, total - one])
    lengths = jnp.asarray(split_up(count, total, most, slope), jnp.int32)
    twos = (count - 1) // 2
    giver, receiver = lengths[1:1 + 2 * twos:2], lengths[2:2 + 2 * twos:2]
    margin = jnp.minimum(giver - 1, most - receiver)
    passed = jax.random.randint(jax.random.fold_in(own_key, 1), (twos,), 0, 1 << 20) % (margin + 1)
    lengths = lengths.at[1:1 + 2 * twos:2].set(giver - passed).at[2:2 + 2 * twos:2].set(receiver + passed)
    return lengths[jax.random.permutation(jax.random.fold_in(own_key, 2), count)]


def normal_values(key, dims, spread, bound, split=(), kind=jnp.bfloat16):
    level = shard_levels(key, dims, split, -0.22, 0.18) if split else 1.0
    drawn = jax.random.normal(key, dims, jnp.float32) * spread * level
    return jnp.minimum(jnp.maximum(drawn, -bound), bound).astype(kind)


def setup_inputs(seed: int = 0) -> dict:
    key_of = jax.random.split(jax.random.key(seed), 14)
    frames_in = normal_values(key_of[0], (TOKENS, D), 1.0, 6.0, ((0, 32),), jnp.float32)
    frames_cot = normal_values(key_of[1], (TOKENS, D), 1.0, 6.0, ((0, 32),), jnp.float32)
    clip_ids = jnp.searchsorted(jnp.cumsum(ragged(key_of[2], CLIPS, TOKENS, TOK_DEV, 0)), jnp.arange(TOKENS), side="right").astype(jnp.int32)
    frame_mask = place_ends((jax.random.randint(key_of[3], (TOKENS,), 0, 8) < 7).astype(jnp.int32), jax.random.fold_in(key_of[3], 1), 0, 1)
    norm_gain = jnp.clip(1.0 + 0.15 * jax.random.normal(key_of[4], (LAYERS, 2, D), jnp.float32), 0.25, 1.75)
    norm_bias = normal_values(key_of[5], (LAYERS, 2, D), 0.3, 2.0, (), jnp.float32)
    qkv_weight = draw_qkv_weight(jax.random.fold_in(key_of[13], 71), 0)
    qv_bias = normal_values(key_of[7], (LAYERS, 2, D), 0.05, 0.4, ((2, 2),), jnp.float32)
    proj_weight = normal_values(key_of[8], (LAYERS, D, D), (max(D // 384, 1)) ** -0.5, 4.0, ((1, 32),))
    up_weight = normal_values(key_of[9], (LAYERS, D, FF), D ** -0.5, 0.21875, ((1, 16), (2, 2)))
    up_bias = normal_values(key_of[10], (LAYERS, FF), 0.5, 3.0, ((1, 2),), jnp.float32)
    down_weight = normal_values(key_of[11], (LAYERS, FF, D), FF ** -0.5, 0.109375, ((1, 32),))
    out_biases = normal_values(key_of[12], (LAYERS, 2, D), 0.3, 2.0, (), jnp.float32)
    return {"frames_in": frames_in, "frames_cot": frames_cot, "clip_ids": clip_ids, "frame_mask": frame_mask, "norm_gain": norm_gain, "norm_bias": norm_bias, "qkv_weight": qkv_weight, "qv_bias": qv_bias, "proj_weight": proj_weight, "up_weight": up_weight, "up_bias": up_bias, "down_weight": down_weight, "out_biases": out_biases}


epsilon = 1e-05

def norm_forward(values, gain_vec, bias_vec):
    row_mean = lax.optimization_barrier(jnp.mean(values, axis=-1, keepdims=True))
    centred = values - row_mean
    inverse = lax.rsqrt(lax.optimization_barrier(jnp.mean(centred * centred, axis=-1, keepdims=True)) + epsilon)
    normed = centred * inverse
    return ((normed * gain_vec + bias_vec).astype(jnp.bfloat16), normed, inverse)

def norm_backward(grad_out, normed, inverse, gain_vec):
    scaled = grad_out * gain_vec
    projected = scaled - lax.optimization_barrier(jnp.mean(scaled, axis=-1, keepdims=True)) - normed * lax.optimization_barrier(jnp.mean(scaled * normed, axis=-1, keepdims=True))
    return (inverse * projected, lax.optimization_barrier(jnp.sum(grad_out * normed, axis=0)), lax.optimization_barrier(jnp.sum(grad_out, axis=0)))

def gelu_value(preact):
    return 0.5 * preact * (1.0 + jax.scipy.special.erf(preact * 0.7071067811865476))

def gelu_slope(preact):
    return 0.5 * (1.0 + jax.scipy.special.erf(preact * 0.7071067811865476)) + preact * jnp.exp(-0.5 * preact * preact) * 0.3989422804014327

def rounded(values):
    return lax.optimization_barrier(values.astype(jnp.bfloat16)).astype(jnp.float32)

def padded(values, tok_span, fill):
    border = jnp.full((tok_span,) + values.shape[1:], fill, values.dtype)
    return jnp.concatenate([border, values, border], axis=0)

def block_mask(query_ids, block_start, key_ids, key_valid, tok_span):
    query_pos = block_start + jnp.arange(query_ids.shape[0], dtype=jnp.int32)
    key_pos = jnp.arange(key_ids.shape[0], dtype=jnp.int32)
    same_clip = query_ids[:, None] == key_ids[None, :]
    visible = (key_valid[None, :] == 1) | (key_pos[None, :] == query_pos[:, None] + tok_span)
    return same_clip & visible

def block_inputs(query, key_pad, value_pad, ids_pad, valid_pad, offset, tok_span):
    query_block = lax.dynamic_slice_in_dim(query, offset, tok_span, 0).astype(jnp.float32)
    key_block = lax.dynamic_slice_in_dim(key_pad, offset, 3 * tok_span, 0).astype(jnp.float32)
    value_block = lax.dynamic_slice_in_dim(value_pad, offset, 3 * tok_span, 0).astype(jnp.float32)
    allowed = block_mask(lax.dynamic_slice_in_dim(ids_pad, offset + tok_span, tok_span, 0), 0, lax.dynamic_slice_in_dim(ids_pad, offset, 3 * tok_span, 0), lax.dynamic_slice_in_dim(valid_pad, offset, 3 * tok_span, 0), tok_span)
    scores = jnp.einsum('qhd,khd->hqk', query_block, key_block) * HD ** (-0.5)
    scores = jnp.where(allowed[None], scores, -1e+30)
    return (query_block, key_block, value_block, scores)

def attention_forward(query, keys, values, clip_ids, frame_mask):
    tok_span = TOK_DEV
    key_pad = padded(keys, tok_span, 0)
    value_pad = padded(values, tok_span, 0)
    ids_pad = padded(clip_ids, tok_span, -1)
    valid_pad = padded(frame_mask, tok_span, 0)

    def one_block(block_id):
        offset = block_id * tok_span
        query_block, key_block, value_block, scores = block_inputs(query, key_pad, value_pad, ids_pad, valid_pad, offset, tok_span)
        row_max = lax.optimization_barrier(jnp.max(scores, axis=-1, keepdims=True))
        log_total = row_max + jnp.log(lax.optimization_barrier(jnp.sum(jnp.exp(scores - row_max), axis=-1, keepdims=True)))
        prob_low = rounded(jnp.exp(scores - log_total))
        attended = jnp.einsum('hqk,khd->qhd', prob_low, value_block).astype(jnp.bfloat16)
        return (attended, log_total[..., 0])
    attended, log_totals = lax.map(one_block, jnp.arange(query.shape[0] // tok_span, dtype=jnp.int32))
    return (attended.reshape(query.shape), log_totals)

def attention_backward(query, keys, values, attended, grad_attn, log_totals, clip_ids, frame_mask):
    tok_span = TOK_DEV
    key_pad = padded(keys, tok_span, 0)
    value_pad = padded(values, tok_span, 0)
    ids_pad = padded(clip_ids, tok_span, -1)
    valid_pad = padded(frame_mask, tok_span, 0)
    score_scale = HD ** (-0.5)

    def one_block(key_grads, block_id):
        offset = block_id * tok_span
        query_block, key_block, value_block, scores = block_inputs(query, key_pad, value_pad, ids_pad, valid_pad, offset, tok_span)
        prob_full = jnp.exp(scores - log_totals[block_id][..., None])
        prob_low = rounded(prob_full)
        grad_block = lax.dynamic_slice_in_dim(grad_attn, offset, tok_span, 0).astype(jnp.float32)
        out_block = lax.dynamic_slice_in_dim(attended, offset, tok_span, 0).astype(jnp.float32)
        grad_prob = jnp.einsum('qhd,khd->hqk', grad_block, value_block)
        delta_row = lax.optimization_barrier(jnp.sum(grad_block * out_block, axis=-1)).T
        score_low = rounded(prob_full * (grad_prob - delta_row[..., None]))
        grad_query = jnp.einsum('hqk,khd->qhd', score_low, key_block) * score_scale
        grad_key = jnp.einsum('hqk,qhd->khd', score_low, query_block) * score_scale
        grad_value = jnp.einsum('hqk,qhd->khd', prob_low, grad_block)
        key_value = jnp.stack([grad_key, grad_value], axis=1)
        current = lax.dynamic_slice_in_dim(key_grads, offset, 3 * tok_span, 0)
        key_grads = lax.dynamic_update_slice_in_dim(key_grads, current + key_value, offset, 0)
        return (key_grads, grad_query)
    start = jnp.zeros((query.shape[0] + 2 * tok_span, 2) + query.shape[1:], jnp.float32)
    key_grads, grad_query = lax.scan(one_block, start, jnp.arange(query.shape[0] // tok_span, dtype=jnp.int32))
    return (grad_query.reshape(query.shape), key_grads[tok_span:tok_span + query.shape[0]])

def reference(frames_in, frames_cot, clip_ids, frame_mask, norm_gain, norm_bias, qkv_weight, qv_bias, proj_weight, up_weight, up_bias, down_weight, out_biases):
    row_total = frames_in.shape[0]
    stored_all = []
    state = frames_in
    for depth in range(LAYERS):
        first_norm, hat_one, inv_one = norm_forward(state, norm_gain[depth, 0], norm_bias[depth, 0])
        qkv_flat = qkv_weight[depth].reshape(D, 3 * D)
        bias_three = jnp.stack([qv_bias[depth, 0], jnp.zeros((D,), jnp.float32), qv_bias[depth, 1]])
        qkv_proj = jnp.dot(first_norm, qkv_flat, preferred_element_type=jnp.float32).reshape(row_total, 3, D) + bias_three
        qkv_proj = qkv_proj.astype(jnp.bfloat16)
        query = qkv_proj[:, 0].reshape(row_total, H, HD)
        keys = qkv_proj[:, 1].reshape(row_total, H, HD)
        values = qkv_proj[:, 2].reshape(row_total, H, HD)
        attended, log_totals = attention_forward(query, keys, values, clip_ids, frame_mask)
        attn_flat = attended.reshape(row_total, D)
        middle = state + jnp.dot(attn_flat, proj_weight[depth], preferred_element_type=jnp.float32) + out_biases[depth, 0]
        second_norm, hat_two, inv_two = norm_forward(middle, norm_gain[depth, 1], norm_bias[depth, 1])
        preact = jnp.dot(second_norm, up_weight[depth], preferred_element_type=jnp.float32) + up_bias[depth]
        hidden = gelu_value(preact).astype(jnp.bfloat16)
        state = middle + jnp.dot(hidden, down_weight[depth], preferred_element_type=jnp.float32) + out_biases[depth, 1]
        stored_all.append((first_norm, hat_one, inv_one, query, keys, values, attended, log_totals, hat_two, inv_two, second_norm, preact, hidden))
    frames_out = state
    gradient = frames_cot
    grads_qkv, grads_qv, grads_proj, grads_up, grads_upb, grads_down, grads_gain, grads_nbias, grads_obias = ([], [], [], [], [], [], [], [], [])
    for depth in range(LAYERS - 1, -1, -1):
        first_norm, hat_one, inv_one, query, keys, values, attended, log_totals, hat_two, inv_two, second_norm, preact, hidden = stored_all[depth]
        grad_low = gradient.astype(jnp.bfloat16)
        grad_down = jnp.dot(hidden.T, grad_low, preferred_element_type=jnp.float32)
        grad_pre = jnp.dot(grad_low, down_weight[depth].T, preferred_element_type=jnp.float32) * gelu_slope(preact)
        grad_upb = lax.optimization_barrier(jnp.sum(grad_pre, axis=0))
        pre_low = grad_pre.astype(jnp.bfloat16)
        grad_up = jnp.dot(second_norm.T, pre_low, preferred_element_type=jnp.float32)
        grad_second = jnp.dot(pre_low, up_weight[depth].T, preferred_element_type=jnp.float32)
        back_two, gain_two, shift_two = norm_backward(grad_second, hat_two, inv_two, norm_gain[depth, 1])
        grad_middle = gradient + back_two
        middle_low = grad_middle.astype(jnp.bfloat16)
        attn_flat = attended.reshape(row_total, D)
        grad_proj = jnp.dot(attn_flat.T, middle_low, preferred_element_type=jnp.float32)
        grad_attn = jnp.dot(middle_low, proj_weight[depth].T, preferred_element_type=jnp.float32).astype(jnp.bfloat16)
        grad_query, key_grads = attention_backward(query, keys, values, attended, grad_attn.reshape(row_total, H, HD), log_totals, clip_ids, frame_mask)
        grad_query = grad_query.reshape(row_total, D)
        grad_key = key_grads[:, 0].reshape(row_total, D)
        grad_value = key_grads[:, 1].reshape(row_total, D)
        grad_qv = jnp.stack([lax.optimization_barrier(jnp.sum(grad_query, axis=0)), lax.optimization_barrier(jnp.sum(grad_value, axis=0))])
        qkv_low = jnp.stack([grad_query, grad_key, grad_value], axis=1).astype(jnp.bfloat16).reshape(row_total, 3 * D)
        grad_qkv = jnp.dot(first_norm.T, qkv_low, preferred_element_type=jnp.float32).reshape(D, 3, D)
        grad_first = jnp.dot(qkv_low, qkv_weight[depth].reshape(D, 3 * D).T, preferred_element_type=jnp.float32)
        back_one, gain_one, shift_one = norm_backward(grad_first, hat_one, inv_one, norm_gain[depth, 0])
        grads_obias.insert(0, jnp.stack([lax.optimization_barrier(jnp.sum(grad_middle, axis=0)), lax.optimization_barrier(jnp.sum(gradient, axis=0))]))
        gradient = grad_middle + back_one
        grads_qkv.insert(0, grad_qkv)
        grads_qv.insert(0, grad_qv)
        grads_proj.insert(0, grad_proj)
        grads_up.insert(0, grad_up)
        grads_upb.insert(0, grad_upb)
        grads_down.insert(0, grad_down)
        grads_gain.insert(0, jnp.stack([gain_one, gain_two]))
        grads_nbias.insert(0, jnp.stack([shift_one, shift_two]))
    return (frames_out, gradient, jnp.stack(grads_qkv), jnp.stack(grads_qv), jnp.stack(grads_proj), jnp.stack(grads_up), jnp.stack(grads_upb), jnp.stack(grads_down), jnp.stack(grads_gain), jnp.stack(grads_nbias), jnp.stack(grads_obias))
```

```python
import jax, jax.numpy as jnp, functools
from jax import lax
from jax.experimental import pallas as pl
from jax.experimental.pallas import tpu as pltpu
from jax.sharding import Mesh, PartitionSpec as P
MESH = pl.DeviceIdType.MESH
f32 = jnp.float32
bf16 = jnp.bfloat16
EPS = 1e-05
VMEM = pl.BlockSpec(memory_space=pltpu.VMEM)

def place():
    return tuple(lax.axis_index(n) for n in ("z", "x", "core", "y"))

def chips():
    return lax.axis_size("z") * 4

def gather_kernel(count, y_first, *refs):
    n = len(y_first)
    ins, outs = refs[:n], refs[n+1:2*n+1]
    bias_in, bias_out = refs[n], refs[2*n+1]
    up_sem, down_sem, side_sem, mate_sem, recv_sem, own_send, own_recv, copy_sem, bias_sem = refs[2*n+2:]
    z, x, core, y = place()
    rows = count // 4
    quad = 2 * z + x
    dp = 2 * quad + core
    head = core == y
    sibling = (z, x, 1 - core, y)
    side = (z, 1 - x, core, y)
    above = (z + 1, x, core, y)
    below = (z - 1, x, core, y)
    mate = (z, x, core, 1 - y)
    has_up = z + 1 < rows
    has_down = z > 0
    bar = pltpu.get_barrier_semaphore()
    def sig(dev): pl.semaphore_signal(bar, inc=1, device_id=dev, device_id_type=MESH)
    sig(side)
    @pl.when(has_up)
    def _(): sig(above)
    @pl.when(has_down)
    def _(): sig(below)
    @pl.when(head)
    def _(): sig(sibling)
    @pl.when(jnp.logical_not(head))
    def _(): sig(mate)
    pl.semaphore_wait(bar, 2 + has_up.astype(jnp.int32) + has_down.astype(jnp.int32))

    def piece(m, q, sem, dev):
        part = outs[m].at[pl.ds(2 * q, 2)]
        return pltpu.make_async_remote_copy(part, part, sem.at[m, q], recv_sem.at[m, q], device_id=dev, device_id_type=MESH)

    bias_copy = pltpu.make_async_remote_copy(bias_in, bias_out, bias_sem.at[0], bias_sem.at[1], device_id=mate, device_id_type=MESH)
    @pl.when(head)
    def _():
        bias_copy.start()
        bias_out[...] = bias_in[...]
    @pl.when(jnp.logical_not(head))
    def _():
        for m in range(n):
            pltpu.make_async_remote_copy(ins[m], outs[m].at[dp], own_send.at[m], own_recv.at[m], device_id=sibling, device_id_type=MESH).start()
    def spread(m, q, up, down, across, to_mate):
        @pl.when(up)
        def _(): piece(m, q, up_sem, above).start()
        @pl.when(down)
        def _(): piece(m, q, down_sem, below).start()
        if across: piece(m, q, side_sem, side).start()
        if to_mate: piece(m, q, mate_sem, mate).start()
    def arrive(m, q): piece(m, q, up_sem, above).wait_recv()

    @pl.when(head)
    def _():
        for m in range(n):
            pltpu.make_async_copy(ins[m], outs[m].at[dp], copy_sem.at[m]).start()
        for m in range(n):
            pltpu.make_async_copy(ins[m], outs[m].at[dp], copy_sem.at[m]).wait()
            pltpu.make_async_remote_copy(ins[m], outs[m].at[dp + 1 - 2 * core], own_send.at[m], own_recv.at[m], device_id=sibling, device_id_type=MESH).wait_recv()
            spread(m, quad, has_up, has_down, True, True)

    def line(ms, last):
        def step(k, _):
            for m in ms:
                @pl.when(z - k >= 0)
                def _():
                    q = quad - 2 * k
                    arrive(m, q)
                    spread(m, q, has_up, False, True, last)
                @pl.when(z + k < rows)
                def _():
                    q = quad + 2 * k
                    arrive(m, q)
                    spread(m, q, False, has_down, True, last)
                if last:
                    @pl.when(z - k + 1 >= 0)
                    def _():
                        q = side_quad - 2 * (k - 1)
                        arrive(m, q)
                        spread(m, q, False, False, False, True)
                    @pl.when((z + k - 1 < rows) & (k > 1))
                    def _():
                        q = side_quad + 2 * (k - 1)
                        arrive(m, q)
                        spread(m, q, False, False, False, True)
            return 0
        lax.fori_loop(1, rows + (1 if last else 0), step, 0)
    side_quad = quad + 1 - 2 * x
    first = [m for m in range(n) if y_first[m]]
    later = [m for m in range(n) if not y_first[m]]
    @pl.when(head)
    def _():
        line(first, False)
        line(later, True)
    @pl.when(jnp.logical_not(head))
    def _():
        for m in first:
            arrive(m, quad)
            spread(m, quad, has_up, has_down, True, False)
        line(first, False)
        def step(q, _):
            for m in later: arrive(m, q)
            return 0
        lax.fori_loop(0, count // 2, step, 0)
    def step(k, _):
        for m in first: arrive(m, 2 * k + 1 - x)
        return 0
    lax.fori_loop(0, rows, step, 0)
    @pl.when(head)
    def _(): bias_copy.wait_send()
    @pl.when(jnp.logical_not(head))
    def _(): bias_copy.wait_recv()
    def step(k, _):
        for m in range(n):
            fam = head if not y_first[m] else True
            @pl.when(fam & (k <= z) & has_up)
            def _(): piece(m, 2 * k + x, up_sem, above).wait_send()
            @pl.when(fam & (k >= z) & has_down)
            def _(): piece(m, 2 * k + x, down_sem, below).wait_send()
            @pl.when(fam)
            def _(): piece(m, 2 * k + x, side_sem, side).wait_send()
            if not y_first[m]:
                @pl.when(head)
                def _():
                    piece(m, 2 * k, mate_sem, mate).wait_send()
                    piece(m, 2 * k + 1, mate_sem, mate).wait_send()
            else:
                @pl.when(head & (k == z))
                def _(): piece(m, quad, mate_sem, mate).wait_send()
        return 0
    lax.fori_loop(0, rows, step, 0)
    @pl.when(jnp.logical_not(head))
    def _():
        for m in range(n):
            pltpu.make_async_remote_copy(ins[m], outs[m].at[dp], own_send.at[m], own_recv.at[m], device_id=sibling, device_id_type=MESH).wait_send()

def gather(shards, bias, y_first, cid):
    count = chips()
    n = len(shards)
    dma = pltpu.SemaphoreType.DMA
    return pl.pallas_call(
        functools.partial(gather_kernel, count, y_first),
        out_shape=[jax.ShapeDtypeStruct((count,) + s.shape, s.dtype) for s in shards] + [jax.ShapeDtypeStruct(bias.shape, f32)],
        in_specs=[VMEM] * (n + 1),
        out_specs=[pl.BlockSpec(memory_space=pl.ANY)] * n + [VMEM],
        scratch_shapes=[dma((n, count // 2))] * 5 + [dma((n,))] * 3 + [dma((2,))],
        compiler_params=pltpu.CompilerParams(collective_id=cid, has_side_effects=True),
    )(*shards, bias)

def rcopy(src, dst, send, recv, dev):
    return pltpu.make_async_remote_copy(src, dst, send, recv, device_id=dev, device_id_type=MESH)

def ready(devs):
    bar = pltpu.get_barrier_semaphore()
    for dev, ok in devs:
        if ok is True:
            pl.semaphore_signal(bar, inc=1, device_id=dev, device_id_type=MESH)
        else:
            @pl.when(ok)
            def _(): pl.semaphore_signal(bar, inc=1, device_id=dev, device_id_type=MESH)
    return bar

def as_int(v): return v.astype(jnp.int32)

def halo_kernel(count, a_ref, win, sib_s, mate_s, far_s, recv, own_s):
    z, x, core, y = place()
    quad, quads = 2 * z + x, count // 2
    at_quad = lambda q: (q // 2, lax.rem(q, 2), core, y)
    sibling, mate = (z, x, 1 - core, y), (z, x, core, 1 - y)
    is1 = core == 1
    target, source = at_quad(quad - 1 + 2 * core), at_quad(quad + 1 - 2 * core)
    has_target = jnp.where(is1, quad + 1 < quads, quad > 0)
    has_source = jnp.where(is1, quad > 0, quad + 1 < quads)
    bar = ready([(sibling, True), (mate, True), (source, has_source)])
    own = 2 + 2 * core
    from_mate = 2 * core + 3 - 2 * y
    far = 6 - 6 * core
    passes = (core == y) & has_source
    extra = 5 - 4 * core
    takes = (core != y) & has_source
    @pl.when(quad == 0)
    def _():
        win[0] = jnp.zeros_like(win[0])
        @pl.when(y == 0)
        def _(): win[1] = jnp.zeros_like(win[1])
    @pl.when(quad == quads - 1)
    def _():
        win[6] = jnp.zeros_like(win[6])
        @pl.when(y == 1)
        def _(): win[5] = jnp.zeros_like(win[5])
    pl.semaphore_wait(bar, 2 + as_int(has_target))
    to_far = rcopy(a_ref, win.at[far], far_s.at[0], recv.at[far], target)
    to_mate = rcopy(a_ref, win.at[2 * core + 1 + 2 * y], mate_s.at[0], recv.at[2 * core + 1 + 2 * y], mate)
    to_sib = rcopy(a_ref, win.at[own], sib_s.at[own], recv.at[own], sibling)
    on = lambda w: rcopy(win.at[w], win.at[w], sib_s.at[w], recv.at[w], sibling)
    hand = rcopy(win.at[far], win.at[extra], mate_s.at[1], recv.at[extra], mate)
    @pl.when(has_target)
    def _(): to_far.start()
    to_mate.start()
    to_sib.start()
    win[own] = a_ref[...]
    on(from_mate).wait_recv()
    on(from_mate).start()
    @pl.when(has_source)
    def _():
        on(far).wait_recv()
        @pl.when(passes)
        def _(): hand.start()
        on(far).start()
    @pl.when(takes)
    def _():
        on(extra).wait_recv()
        on(extra).start()
    oc = 1 - core
    on(2 + 2 * oc).wait_recv()
    on(2 * oc + 3 - 2 * y).wait_recv()
    sib_source = jnp.where(is1, quad + 1 < quads, quad > 0)
    @pl.when(sib_source)
    def _():
        on(6 - 6 * oc).wait_recv()
    @pl.when(sib_source & (oc != y))
    def _(): on(5 - 4 * oc).wait_recv()
    @pl.when(has_target)
    def _(): to_far.wait_send()
    to_mate.wait_send()
    to_sib.wait_send()
    on(from_mate).wait_send()
    @pl.when(has_source)
    def _(): on(far).wait_send()
    @pl.when(passes)
    def _(): hand.wait_send()
    @pl.when(takes)
    def _(): on(extra).wait_send()

def halo(a, cid):
    count = chips()
    dma = pltpu.SemaphoreType.DMA
    return pl.pallas_call(
        functools.partial(halo_kernel, count),
        out_shape=jax.ShapeDtypeStruct((7,) + a.shape, a.dtype),
        in_specs=[VMEM], out_specs=VMEM,
        scratch_shapes=[dma((7,)), dma((2,)), dma((1,)), dma((7,)), dma((1,))],
        compiler_params=pltpu.CompilerParams(collective_id=cid, has_side_effects=True, vmem_limit_bytes=60 << 20),
    )(a)

def halo_back_kernel(count, p, out, sib_in, mate_in, far_in, stage, sib_s, sib_r, mate_s, mate_r, far_s, far_r):
    z, x, core, y = place()
    quad, quads = 2 * z + x, count // 2
    at_quad = lambda q: (q // 2, lax.rem(q, 2), core, y)
    sibling, mate = (z, x, 1 - core, y), (z, x, core, 1 - y)
    is1 = core == 1
    source, target = at_quad(quad - 1 + 2 * core), at_quad(quad + 1 - 2 * core)
    has_source = jnp.where(is1, quad + 1 < quads, quad > 0)
    has_target = jnp.where(is1, quad > 0, quad + 1 < quads)
    bar = ready([(sibling, True), (mate, True), (source, has_source)])
    pl.semaphore_wait(bar, 2 + as_int(has_target))
    own = 2 + 2 * core
    to_sib = lambda w: rcopy(p.at[w], sib_in.at[w], sib_s.at[w], sib_r.at[w], sibling)
    oc = 1 - core
    direct = lambda c: 2 * c + 3 - 2 * y
    far = lambda c: 6 - 6 * c
    extra = lambda c: 5 - 4 * c
    gives = (core != y) & has_target
    gets = (core == y) & has_target
    sib_has = has_source
    @pl.when(sib_has & (oc != y))
    def _(): to_sib(extra(oc)).start()
    to_sib(direct(oc)).start()
    @pl.when(sib_has)
    def _(): to_sib(far(oc)).start()
    to_sib(2 + 2 * oc).start()
    hand = rcopy(stage.at[0], mate_in.at[0], mate_s.at[0], mate_r.at[0], mate)
    to_mate = rcopy(stage.at[1], mate_in.at[1], mate_s.at[1], mate_r.at[1], mate)
    to_far = rcopy(stage.at[2], far_in, far_s.at[0], far_r.at[0], target)
    both = lambda w: p[w].astype(f32) + sib_in[w].astype(f32)
    @pl.when(gives)
    def _():
        to_sib(extra(core)).wait_recv()
        stage[0] = both(extra(core)).astype(bf16)
        hand.start()
    to_sib(direct(core)).wait_recv()
    stage[1] = both(direct(core)).astype(bf16)
    to_mate.start()
    @pl.when(has_target)
    def _():
        to_sib(far(core)).wait_recv()
        @pl.when(gets)
        def _():
            hand.wait_recv()
            stage[2] = (both(far(core)) + mate_in[0].astype(f32)).astype(bf16)
        @pl.when(core != y)
        def _(): stage[2] = both(far(core)).astype(bf16)
        to_far.start()
    to_sib(own).wait_recv()
    to_mate.wait_recv()
    out[...] = both(own) + mate_in[1].astype(f32)
    @pl.when(has_source)
    def _():
        to_far.wait_recv()
        out[...] = out[...] + far_in[...].astype(f32)
    @pl.when(sib_has & (oc != y))
    def _(): to_sib(extra(oc)).wait_send()
    to_sib(direct(oc)).wait_send()
    @pl.when(sib_has)
    def _(): to_sib(far(oc)).wait_send()
    to_sib(2 + 2 * oc).wait_send()
    @pl.when(gives)
    def _(): hand.wait_send()
    to_mate.wait_send()
    @pl.when(has_target)
    def _(): to_far.wait_send()

def halo_back(p, cid):
    count = chips()
    dma = pltpu.SemaphoreType.DMA
    one = p.shape[1:]
    return pl.pallas_call(
        functools.partial(halo_back_kernel, count),
        out_shape=jax.ShapeDtypeStruct(one, f32),
        in_specs=[VMEM], out_specs=VMEM,
        scratch_shapes=[pltpu.VMEM((7,) + one, bf16), pltpu.VMEM((2,) + one, bf16), pltpu.VMEM(one, bf16), pltpu.VMEM((3,) + one, bf16),
                        dma((7,)), dma((7,)), dma((2,)), dma((2,)), dma((1,)), dma((1,))],
        compiler_params=pltpu.CompilerParams(collective_id=cid, has_side_effects=True, vmem_limit_bytes=60 << 20),
    )(p)

def pair_gather_kernel(a_ref, out, send, recv):
    z, x, core, y = place()
    sibling = (z, x, 1 - core, y)
    pl.semaphore_wait(ready([(sibling, True)]), 1)
    copy = rcopy(a_ref, out.at[core], send, recv, sibling)
    copy.start()
    out[core] = a_ref[...]
    copy.wait()

def pair_gather(a, cid):
    return pl.pallas_call(
        pair_gather_kernel, out_shape=jax.ShapeDtypeStruct((2,) + a.shape, a.dtype), in_specs=[VMEM], out_specs=VMEM,
        scratch_shapes=[pltpu.SemaphoreType.DMA, pltpu.SemaphoreType.DMA],
        compiler_params=pltpu.CompilerParams(collective_id=cid, has_side_effects=True),
    )(a)

def pair_sum_kernel(p_ref, out, got, send, recv):
    z, x, core, y = place()
    sibling = (z, x, 1 - core, y)
    pl.semaphore_wait(ready([(sibling, True)]), 1)
    copy = rcopy(p_ref.at[1 - core], got, send, recv, sibling)
    copy.start()
    copy.wait()
    out[...] = p_ref[core] + got[...]

def pair_sum(p, cid):
    return pl.pallas_call(
        pair_sum_kernel, out_shape=jax.ShapeDtypeStruct(p.shape[1:], p.dtype), in_specs=[VMEM], out_specs=VMEM,
        scratch_shapes=[pltpu.VMEM(p.shape[1:], p.dtype), pltpu.SemaphoreType.DMA, pltpu.SemaphoreType.DMA],
        compiler_params=pltpu.CompilerParams(collective_id=cid, has_side_effects=True),
    )(p)


def reduce_kernel(count, early, *refs):
    n = len(early)
    rows = count // 4
    grads, outs = refs[:n], refs[n:2*n]
    k = 2*n
    mate_in, side_out, side_in, line_out, up_in, down_in, final_out = [refs[k+i*n:k+(i+1)*n] for i in range(7)]
    k += 7*n
    (mate_s, mate_r, side_s, side_r, up_s, up_r, down_s, down_r, last_s, last_r) = refs[k:]
    z, x, core, y = place()
    quad = 2 * z + x
    dp = 2 * quad + core
    head = core == y
    other = jnp.logical_not(head)
    sibling = (z, x, 1 - core, y)
    side = (z, 1 - x, core, y)
    above = (z + 1, x, core, y)
    below = (z - 1, x, core, y)
    mate = (z, x, core, 1 - y)
    has_up = z + 1 < rows
    has_down = z > 0
    for m in range(n):
        @pl.when(z == 0)
        def _(): up_in[m][...] = jnp.zeros_like(up_in[m])
        @pl.when(z == rows - 1)
        def _(): down_in[m][...] = jnp.zeros_like(down_in[m])
    bar = pltpu.get_barrier_semaphore()
    def sig(dev): pl.semaphore_signal(bar, inc=1, device_id=dev, device_id_type=MESH)
    sig(side)
    @pl.when(has_up)
    def _(): sig(above)
    @pl.when(has_down)
    def _(): sig(below)
    @pl.when(head)
    def _(): sig(mate)
    @pl.when(other)
    def _(): sig(sibling)
    pl.semaphore_wait(bar, 2 + has_up.astype(jnp.int32) + has_down.astype(jnp.int32))

    def rc(src, dst, s, r, dev):
        return pltpu.make_async_remote_copy(src, dst, s, r, device_id=dev, device_id_type=MESH)
    def to_mate(m, q):
        return rc(grads[m].at[pl.ds(2*q, 2)], mate_in[m].at[pl.ds(2*q, 2)], mate_s.at[m, q], mate_r.at[m, q], mate)
    def to_side(m, j):
        return rc(side_out[m].at[j], side_in[m].at[j], side_s.at[m, j], side_r.at[m, j], side)
    def to_up(m, j):
        return rc(line_out[m].at[j], up_in[m].at[j], up_s.at[m, j], up_r.at[m, j], above)
    def to_down(m, j):
        return rc(line_out[m].at[j], down_in[m].at[j], down_s.at[m, j], down_r.at[m, j], below)
    def late_mate(m):
        return rc(line_out[m].at[z], mate_in[m], mate_s.at[m, quad], mate_r.at[m, quad], mate)
    def last(m):
        return rc(final_out[m], outs[m], last_s.at[m], last_r.at[m], sibling)

    def far_first(fn):
        def step(i, _):
            d = rows - i
            for j, ok in ((z + d, z + d < rows), (z - d, z - d >= 0)):
                @pl.when(ok)
                def _(): fn(j)
            return 0
        lax.fori_loop(1, rows, step, 0)
        fn(z)

    order = [m for m in range(n) if early[m]], [m for m in range(n) if not early[m]]

    @pl.when(other)
    def _():
        def go(j):
            for m in order[0]:
                to_mate(m, 2 * j + 1 - x).start()
        def go2(j):
            for m in order[0]:
                to_mate(m, 2 * j + x).start()
        far_first(go); far_first(go2)

    def own(m, q, c, with_mate):
        t = grads[m][2*q+c].astype(f32)
        return t + mate_in[m][2*q+c].astype(f32) if with_mate else t

    def side_stage(ms, with_mate):
        def go(j):
            q = 2 * j + 1 - x
            for m in ms:
                if with_mate: to_mate(m, q).wait_recv()
                def half(c, _):
                    side_out[m][j, c] = own(m, q, c, with_mate).astype(bf16)
                    return 0
                lax.fori_loop(0, 2, half, 0)
            for m in ms:
                to_side(m, j).start()
        far_first(go)

    def line_stage(ms, with_mate):
        def go(j):
            q = 2 * j + x
            for m in ms:
                if with_mate: to_mate(m, q).wait_recv()
                to_side(m, j).wait_recv()
                @pl.when((j >= z) & has_down)
                def _(): to_up(m, j).wait_recv()
                @pl.when((j <= z) & has_up)
                def _(): to_down(m, j).wait_recv()
                def half(c, _):
                    t = own(m, q, c, with_mate) + side_in[m][j, c].astype(f32)
                    @pl.when(j > z)
                    def _(): line_out[m][j, c] = (t + up_in[m][j, c].astype(f32)).astype(bf16)
                    @pl.when(j < z)
                    def _(): line_out[m][j, c] = (t + down_in[m][j, c].astype(f32)).astype(bf16)
                    @pl.when(j == z)
                    def _():
                        u = t + up_in[m][j, c].astype(f32) + down_in[m][j, c].astype(f32)
                        if with_mate:
                            @pl.when(c == core)
                            def _(): outs[m][...] = u
                            @pl.when(c != core)
                            def _(): final_out[m][...] = u
                        else:
                            @pl.when(other)
                            def _(): line_out[m][j, c] = u.astype(bf16)
                            @pl.when(head & (c == core))
                            def _(): outs[m][...] = u
                            @pl.when(head & (c != core))
                            def _(): final_out[m][...] = u
                    return 0
                lax.fori_loop(0, 2, half, 0)
            for m in ms:
                @pl.when(j > z)
                def _(): to_up(m, j).start()
                @pl.when(j < z)
                def _(): to_down(m, j).start()
        far_first(go)

    side_stage(order[1], False)
    @pl.when(head)
    def _(): side_stage(order[0], True)
    line_stage(order[1], False)
    @pl.when(other)
    def _():
        for m in order[1]: late_mate(m).start()
    @pl.when(head)
    def _():
        line_stage(order[0], True)
        for m in order[1]:
            late_mate(m).wait_recv()
            outs[m][...] = outs[m][...] + mate_in[m][core].astype(f32)
            final_out[m][...] = final_out[m][...] + mate_in[m][1 - core].astype(f32)
        for m in range(n):
            last(m).start()
    @pl.when(other)
    def _():
        for m in range(n): last(m).wait_recv()
    def step(j, _):
        for m in range(n):
            fam = head if early[m] else True
            @pl.when(fam)
            def _(): to_side(m, j).wait_send()
            @pl.when(fam & (j > z))
            def _(): to_up(m, j).wait_send()
            @pl.when(fam & (j < z))
            def _(): to_down(m, j).wait_send()
            if early[m]:
                @pl.when(other)
                def _():
                    to_mate(m, 2 * j).wait_send()
                    to_mate(m, 2 * j + 1).wait_send()
        return 0
    lax.fori_loop(0, rows, step, 0)
    for m in range(n):
        @pl.when(head)
        def _(): last(m).wait_send()
        if not early[m]:
            @pl.when(other)
            def _(): late_mate(m).wait_send()

def scatter_sum(grads, early, cid):
    count = chips()
    n = len(grads)
    rows = count // 4
    dma = pltpu.SemaphoreType.DMA
    quads = [pltpu.VMEM((rows, 2) + g.shape[1:], bf16) for g in grads]
    mates = [pltpu.VMEM(((count if e else 2),) + g.shape[1:], bf16) for g, e in zip(grads, early)]
    lasts = [pltpu.VMEM(g.shape[1:], f32) for g in grads]
    return pl.pallas_call(
        functools.partial(reduce_kernel, count, early),
        out_shape=[jax.ShapeDtypeStruct(g.shape[1:], f32) for g in grads],
        in_specs=[pl.BlockSpec(memory_space=pltpu.VMEM)] * n,
        out_specs=[pl.BlockSpec(memory_space=pltpu.VMEM)] * n,
        scratch_shapes=mates + quads * 5 + lasts + [dma((n, count // 2))] * 2 + [dma((n, rows))] * 6 + [dma((n,))] * 2,
        compiler_params=pltpu.CompilerParams(collective_id=cid, has_side_effects=True, vmem_limit_bytes=60 << 20),
    )(*grads)
TQ, TK, BQ, BK = 384, 512, 384, 512
NEG = -1e30

def nt(a, b):
    return lax.dot_general(a, b, (((1,), (1,)), ((), ())), preferred_element_type=f32)
def tn(a, b):
    return lax.dot_general(a, b, (((0,), (0,)), ((), ())), preferred_element_type=f32)

def fold(t, op):
    out = t[:, :128]
    for i in range(1, t.shape[1] // 128):
        out = op(out, t[:, i*128:(i+1)*128])
    return out

def tiled(t, n):
    return t if n == 128 else jnp.concatenate([t] * (n // 128), axis=1)

def tile_at(lo, j, size, wide):
    want = lo + j * size
    start = jnp.minimum(want, wide - size)
    return pl.multiple_of(start, 128), want - start

def fwd_kernel(half, span_ref, q_ref, k_ref, v_ref, idq_ref, idk_ref, o_ref, lse_ref, s_scr, m_scr, l_scr, acc):
    i = pl.program_id(0)
    T = q_ref.shape[0]
    pairs = q_ref.shape[1] // 128
    wide = k_ref.shape[0]
    lo, steps = span_ref[0, i], span_ref[1, i]
    low = lax.broadcasted_iota(jnp.int32, (T, 128), 1) < 64
    qs = []
    for p in range(pairs):
        qp = q_ref[:, p*128:(p+1)*128] * jnp.bfloat16(0.125)
        z = jnp.zeros_like(qp)
        qs += [jnp.where(low, qp, z), jnp.where(low, z, qp)]
    gap = 2 * half + i * T + jnp.where(i >= half // T, half, 0)
    idq = idq_ref[...]
    col = lax.broadcasted_iota(jnp.int32, (T, TK), 1)
    rel = col - lax.broadcasted_iota(jnp.int32, (T, TK), 0)
    for h in range(2 * pairs):
        m_scr[h] = jnp.full((T, 128), NEG, f32)
        l_scr[h] = jnp.zeros((T, 128), f32)
    for p in range(pairs):
        acc[p] = jnp.zeros((T, 128), f32)
    def scores(j, _):
        start, fresh = tile_at(lo, j, TK, wide)
        ok = ((idq == idk_ref[0:1, pl.ds(start, TK)]) | (rel == gap - start)) & (col >= fresh)
        for h in range(2 * pairs):
            p = h // 2
            s = jnp.where(ok, nt(qs[h], k_ref[pl.ds(start, TK), p*128:(p+1)*128]), NEG)
            s_scr[h, j] = s
            m_scr[h] = jnp.maximum(m_scr[h], fold(s, jnp.maximum))
        return 0
    lax.fori_loop(0, steps, scores, 0)
    for h in range(2 * pairs):
        m_scr[h] = jnp.broadcast_to(jnp.max(m_scr[h], axis=1, keepdims=True), (T, 128))
    def values(j, _):
        start, fresh = tile_at(lo, j, TK, wide)
        for p in range(pairs):
            vp = v_ref[pl.ds(start, TK), p*128:(p+1)*128]
            out = []
            for h in (2*p, 2*p+1):
                e = jnp.exp(s_scr[h, j] - tiled(m_scr[h], TK))
                l_scr[h] = l_scr[h] + fold(e, jnp.add)
                out.append(jnp.dot(e.astype(bf16), vp, preferred_element_type=f32))
            acc[p] = acc[p] + jnp.where(low, out[0], out[1])
        return 0
    lax.fori_loop(0, steps, values, 0)
    for p in range(pairs):
        inv = [1.0 / jnp.sum(l_scr[h], axis=1, keepdims=True) for h in (2*p, 2*p+1)]
        o_ref[:, p*128:(p+1)*128] = (acc[p] * jnp.where(low, inv[0], inv[1])).astype(bf16)
    for h in range(2 * pairs):
        total = jnp.sum(l_scr[h].T, axis=0, keepdims=True)
        lse_ref[h:h+1, :] = m_scr[h].T[0:1, :] + jnp.log(total)

def attend(q, k, v, span, idq, idk):
    rows, cols = q.shape
    wide = k.shape[0]
    heads = cols // 64
    tiles = rows // TQ
    full = lambda a: pl.BlockSpec(a.shape, lambda i, s: (0,) * a.ndim)
    most = (4 * (rows // 2) + TQ + TK) // TK + 1
    return pl.pallas_call(
        functools.partial(fwd_kernel, rows // 2),
        grid_spec=pltpu.PrefetchScalarGridSpec(
            num_scalar_prefetch=1, grid=(tiles,),
            in_specs=[pl.BlockSpec((TQ, cols), lambda i, s: (i, 0)), full(k), full(v),
                      pl.BlockSpec((TQ, 1), lambda i, s: (i, 0)), full(idk)],
            out_specs=[pl.BlockSpec((TQ, cols), lambda i, s: (i, 0)), pl.BlockSpec((heads, TQ), lambda i, s: (0, i))],
            scratch_shapes=[pltpu.VMEM((heads, most, TQ, TK), f32), pltpu.VMEM((heads, TQ, 128), f32), pltpu.VMEM((heads, TQ, 128), f32),
                            pltpu.VMEM((heads // 2, TQ, 128), f32)]),
        out_shape=[jax.ShapeDtypeStruct((rows, cols), bf16), jax.ShapeDtypeStruct((heads, rows), f32)],
        compiler_params=pltpu.CompilerParams(vmem_limit_bytes=60 << 20, dimension_semantics=("arbitrary",)),
        cost_estimate=pl.CostEstimate(flops=4*rows*wide*cols, bytes_accessed=6*wide*cols, transcendentals=0),
    )(span, q, k, v, idq, idk)

def bwd_kernel(half, span_ref, q_ref, k_ref, v_ref, o_ref, da_ref, lse_ref, idq_ref, idk_ref, dq_ref, dk_ref, dv_ref, dk_acc, dv_acc, dq_acc):
    i = pl.program_id(0)
    T = q_ref.shape[0]
    pairs = q_ref.shape[1] // 128
    wide = k_ref.shape[0]
    lo, steps = span_ref[0, i], span_ref[1, i]
    low = lax.broadcasted_iota(jnp.int32, (T, 128), 1) < 64
    @pl.when(i == 0)
    def _():
        dk_acc[...] = jnp.zeros_like(dk_acc)
        dv_acc[...] = jnp.zeros_like(dv_acc)
    qs, das, delta = [], [], []
    for p in range(pairs):
        at = slice(p*128, (p+1)*128)
        qp = q_ref[:, at] * jnp.bfloat16(0.125)
        dp = da_ref[:, at]
        z = jnp.zeros_like(qp)
        qs += [jnp.where(low, qp, z), jnp.where(low, z, qp)]
        das += [jnp.where(low, dp, z), jnp.where(low, z, dp)]
        t = (dp.astype(f32) * o_ref[:, at].astype(f32)).T
        delta += [jnp.sum(t[:64], axis=0, keepdims=True), jnp.sum(t[64:], axis=0, keepdims=True)]
        dq_acc[p] = jnp.zeros((T, 128), f32)
    gap = 2 * half + i * T + jnp.where(i >= half // T, half, 0)
    idq = idq_ref[...]
    row = lax.broadcasted_iota(jnp.int32, (BK, T), 0)
    rel = row - lax.broadcasted_iota(jnp.int32, (BK, T), 1)
    def tile(j, _):
        start, fresh = tile_at(lo, j, BK, wide)
        at_rows = pl.ds(start, BK)
        ok = ((idk_ref[at_rows, :] == idq) | (rel == gap - start)) & (row >= fresh)
        for p in range(pairs):
            at = slice(p*128, (p+1)*128)
            kp, vp = k_ref[at_rows, at], v_ref[at_rows, at]
            kx = kp * jnp.bfloat16(0.125)
            dk = dv = 0
            dq = []
            for h in (2*p, 2*p+1):
                s = jnp.where(ok, nt(kp, qs[h]), NEG)
                pr = jnp.exp(s - lse_ref[h:h+1, :])
                ds = (pr * (nt(vp, das[h]) - delta[h])).astype(bf16)
                dv = dv + jnp.dot(pr.astype(bf16), das[h], preferred_element_type=f32)
                dk = dk + jnp.dot(ds, qs[h], preferred_element_type=f32)
                dq.append(tn(ds, kx))
            dq_acc[p] = dq_acc[p] + jnp.where(low, dq[0], dq[1])
            dk_acc[at_rows, at] = dk_acc[at_rows, at] + dk
            dv_acc[at_rows, at] = dv_acc[at_rows, at] + dv
        return 0
    lax.fori_loop(0, steps, tile, 0)
    for p in range(pairs):
        dq_ref[:, p*128:(p+1)*128] = dq_acc[p].astype(dq_ref.dtype)
    @pl.when(i == pl.num_programs(0) - 1)
    def _():
        dk_ref[...] = dk_acc[...].astype(bf16)
        dv_ref[...] = dv_acc[...].astype(bf16)

def attend_back(q, k, v, o, da, lse, span, idq_row, idk_col):
    rows, cols = q.shape
    wide = k.shape[0]
    heads = cols // 64
    tiles = rows // BQ
    full = lambda a: pl.BlockSpec(a.shape, lambda i, s: (0,) * a.ndim)
    qt = pl.BlockSpec((BQ, cols), lambda i, s: (i, 0))
    return pl.pallas_call(
        functools.partial(bwd_kernel, rows // 2),
        grid_spec=pltpu.PrefetchScalarGridSpec(
            num_scalar_prefetch=1, grid=(tiles,),
            in_specs=[qt, full(k), full(v), qt, qt, pl.BlockSpec((heads, BQ), lambda i, s: (0, i)),
                      pl.BlockSpec((1, BQ), lambda i, s: (0, i)), full(idk_col)],
            out_specs=[qt, full(k), full(v)],
            scratch_shapes=[pltpu.VMEM((wide, cols), f32), pltpu.VMEM((wide, cols), f32), pltpu.VMEM((heads // 2, BQ, 128), f32)]),
        out_shape=[jax.ShapeDtypeStruct((rows, cols), bf16), jax.ShapeDtypeStruct((wide, cols), bf16), jax.ShapeDtypeStruct((wide, cols), bf16)],
        compiler_params=pltpu.CompilerParams(vmem_limit_bytes=60 << 20, dimension_semantics=("arbitrary",)),
        cost_estimate=pl.CostEstimate(flops=10*rows*wide*cols, bytes_accessed=10*wide*cols, transcendentals=0),
    )(span, q, k, v, o, da, lse, idq_row, idk_col)

def spans(ids, mine, tq, tk):
    first, final = mine[::tq], mine[tq-1::tq]
    lo = jnp.sum((ids[None, :] < first[:, None]).astype(jnp.int32), axis=1) // 128 * 128
    hi = jnp.sum((ids[None, :] <= final[:, None]).astype(jnp.int32), axis=1)
    return jnp.stack([lo, (hi - lo + tk - 1) // tk])

def window_ids(clip_ids, frame_mask, half):
    z, x, core, y = place()
    start = (4 * (2 * z + x) + y) * half
    pad = 4 * half
    ids = jnp.pad(clip_ids, (2 * half, pad), constant_values=((-1, 1 << 30),))
    val = jnp.pad(frame_mask, (2 * half, pad))
    ids = lax.dynamic_slice_in_dim(ids, start, 7 * half)
    val = lax.dynamic_slice_in_dim(val, start, 7 * half)
    mine = jnp.concatenate([ids[2*half:3*half], ids[4*half:5*half]])
    keys = jnp.where(val == 1, ids, -2)
    return spans(ids, mine, TQ, TK), spans(ids, mine, BQ, BK), mine, keys

def norm_forward(values, gain_vec, bias_vec):
    row_mean = jnp.mean(values, axis=-1, keepdims=True)
    centred = values - row_mean
    inverse = lax.rsqrt(jnp.mean(centred * centred, axis=-1, keepdims=True) + EPS)
    normed = centred * inverse
    return ((normed * gain_vec + bias_vec).astype(bf16), normed, inverse)

def norm_backward(grad_out, normed, inverse, gain_vec):
    scaled = grad_out * gain_vec
    projected = (scaled - jnp.mean(scaled, axis=-1, keepdims=True)
                 - normed * jnp.mean(scaled * normed, axis=-1, keepdims=True))
    return (inverse * projected, jnp.sum(grad_out * normed, axis=0), jnp.sum(grad_out, axis=0))

def gelu_parts(z):
    half = 0.5 * (1.0 + jax.scipy.special.erf(z * 0.7071067811865476))
    return z * half, half + z * jnp.exp(-0.5 * z * z) * 0.3989422804014327

def mm(a, b):
    return jnp.dot(a, b, preferred_element_type=f32)

def pack(parts, width):
    return jnp.concatenate([p[..., i:i + width] for p in parts for i in range(0, p.shape[-1], width)], axis=1)

def unpack(packed, shapes, width):
    out, at = [], 0
    for r, c in shapes:
        n = c // width
        out.append(jnp.concatenate([packed[:, at + i * r:at + (i + 1) * r] for i in range(n)], axis=-1))
        at += n * r
    return out

def swap(t):
    return lax.ppermute(t, ("core", "y"), [(0, 0), (1, 2), (2, 1), (3, 3)])

def body(frames_in, frames_cot, clip_ids, frame_mask, norm_gain, norm_bias, qkv_weight, qv_bias,
         proj_weight, up_weight, up_bias, down_weight, out_biases):
    layers = qkv_weight.shape[0]
    half, width = frames_in.shape
    z, x, core, y = place()
    count = chips()
    group = ("z", "x", "y")
    hcols = qkv_weight.shape[-1]
    hidden = up_weight.shape[-1]
    span, span_back, mine, keys = window_ids(clip_ids, frame_mask, half)
    idk = keys[None, :]
    shards = [[qkv_weight[l].reshape(-1, 3 * hcols), proj_weight[l], up_weight[l], down_weight[l]] for l in range(layers)]
    bias = jnp.concatenate([up_bias, qv_bias.reshape(layers, 2 * hcols)], axis=1)
    moved = swap(pack([s[None] for s in shards[1]], hcols)[0])
    *full, bias = gather(shards[0], bias, [False, True, True, False], 0)
    full = [[w.reshape(-1, w.shape[-1]) for w in full]]
    moved, full[0] = lax.optimization_barrier((moved, full[0]))
    both = lax.all_gather(moved, group, axis=0, tiled=False)
    full.append([w.reshape(-1, w.shape[-1]) for w in unpack(both, [s.shape for s in shards[1]], hcols)])
    state = frames_in
    kept = []
    for l in range(layers):
        wqkv, wproj, wup, wdown = full[l]
        upb, qb, vb = bias[l, :hidden], bias[l, hidden:hidden+hcols], bias[l, hidden+hcols:]
        a, hat1, inv1 = norm_forward(state, norm_gain[l, 0], norm_bias[l, 0])
        win = halo(a, 1)
        a_own = jnp.concatenate([win[2], win[4]])
        a_win = win.reshape(-1, width)
        q = (mm(a_own, wqkv[:, :hcols]) + qb).astype(bf16)
        k = mm(a_win, wqkv[:, hcols:2*hcols]).astype(bf16)
        v = (mm(a_win, wqkv[:, 2*hcols:]) + vb).astype(bf16)
        o, lse = attend(q, k, v, span, mine[:, None], idk)
        middle = state + pair_sum(mm(o, wproj).reshape(2, half, width), 2) + out_biases[l, 0]
        c, hat2, inv2 = norm_forward(middle, norm_gain[l, 1], norm_bias[l, 1])
        c_full = pair_gather(c, 3).reshape(2 * half, width)
        zz = mm(c_full, wup) + upb
        g, slope = gelu_parts(zz)
        g, slope = g.astype(bf16), slope.astype(bf16)
        state = middle + pair_sum(mm(g, wdown).reshape(2, half, width), 2) + out_biases[l, 1]
        kept.append((a_own, a_win, hat1, inv1, q, k, v, o, lse, hat2, inv2, c_full, g, slope))
    grad = frames_cot
    wgrads, small = [None] * layers, [None] * layers
    for l in reversed(range(layers)):
        wqkv, wproj, wup, wdown = full[l]
        a_own, a_win, hat1, inv1, q, k, v, o, lse, hat2, inv2, c_full, g, slope = kept[l]
        e_full = pair_gather(grad.astype(bf16), 3).reshape(2 * half, width)
        g_down = mm(g.T, e_full)
        dz = mm(e_full, wdown.T) * slope.astype(f32)
        upb = jnp.sum(dz, axis=0)
        dzb = dz.astype(bf16)
        g_up = mm(c_full.T, dzb)
        dc = pair_sum(mm(dzb, wup.T).reshape(2, half, width), 2)
        back, gain2, shift2 = norm_backward(dc, hat2, inv2, norm_gain[l, 1])
        dh = grad + back
        dh_full = pair_gather(dh.astype(bf16), 3).reshape(2 * half, width)
        g_proj = mm(o.T, dh_full)
        da = mm(dh_full, wproj.T).astype(bf16)
        dq, dk, dv = attend_back(q, k, v, o, da, lse, span_back, mine[None, :], keys[:, None])
        qb = jnp.sum(dq.astype(f32), axis=0)
        vb = jnp.sum(dv.astype(f32), axis=0)
        g_qkv = jnp.concatenate([mm(a_own.T, dq), mm(a_win.T, dk), mm(a_win.T, dv)], axis=1)
        wq, wk, wv = wqkv[:, :hcols], wqkv[:, hcols:2*hcols], wqkv[:, 2*hcols:]
        part = mm(dk, wk.T) + mm(dv, wv.T)
        part = part.reshape(7, half, width)
        pq = mm(dq, wq.T).reshape(2, half, width)
        part = jnp.stack([part[0], part[1], part[2] + pq[0], part[3], part[4] + pq[1], part[5], part[6]]).astype(bf16)
        da1 = halo_back(part, 4)
        back, gain1, shift1 = norm_backward(da1, hat1, inv1, norm_gain[l, 0])
        parts = [jnp.stack([gain1, gain2]), jnp.stack([shift1, shift2]),
                 jnp.stack([jnp.sum(dh, axis=0), jnp.sum(grad, axis=0)])]
        grad = dh + back
        wide = lambda t, n: lax.dynamic_update_slice_in_dim(jnp.zeros(t.shape[:-1] + (n,), f32), t, core * t.shape[-1], t.ndim - 1)
        parts += [wide(jnp.stack([qb, vb]), 2 * hcols), wide(upb, 2 * hidden)]
        small[l] = parts
        grads = [t.astype(bf16).reshape(count, -1, t.shape[-1]) for t in (g_qkv, g_proj, g_up, g_down)]
        if l == 0:
            wgrads[l] = scatter_sum(grads, [False, True, False, True], 5)
        else:
            packed = pack(grads, hcols)
            packed, grad = lax.optimization_barrier((packed, grad))
            rows = packed.shape[1]
            own = lax.psum_scatter(packed.reshape(-1, hcols), group, scatter_dimension=0, tiled=True)
            wgrads[l] = [w[0] for w in unpack(swap(own)[None].astype(f32), [s.shape for s in shards[1]], hcols)]
    flat = jnp.concatenate([t.reshape(-1) for p in small for t in p])
    flat, arrived = lax.optimization_barrier((flat, own))
    flat = lax.psum(flat, ("z", "x", "core", "y"))
    outs, at = [], 0
    for p in small:
        got = []
        for t in p:
            got.append(flat[at:at + t.size].reshape(t.shape)); at += t.size
        outs.append(got)
    gains, shifts, obias, qvb, upb = [jnp.stack([o[i] for o in outs]) for i in range(5)]
    qvb = lax.dynamic_slice_in_dim(qvb, y * hcols, hcols, 2)
    upb = lax.dynamic_slice_in_dim(upb, y * hidden, hidden, 1)
    gq, gp, gu, gd = [jnp.stack([w[i] for w in wgrads]) for i in range(4)]
    return (state, grad, gq.reshape(layers, -1, 3, hcols), qvb, gp, gu, upb, gd, gains, shifts, obias)

def solution(mesh):
    dp, mp = mesh.shape["dp"], mesh.shape["mp"]
    named = Mesh(mesh.devices.reshape(dp // 4, 2, 2, mp), ("z", "x", "core", "y"))
    deep = ("z", "x", "core")
    rows = P(deep + ("y",), None)
    qkv, qv = P(None, deep, None, "y"), P(None, None, "y")
    tall, wide, upb = P(None, ("y",) + deep, None), P(None, deep, "y"), P(None, "y")
    return jax.shard_map(
        body, mesh=named,
        in_specs=(rows, rows, P(), P(), P(), P(), qkv, qv, tall, wide, upb, tall, P()),
        out_specs=(rows, rows, qkv, qv, tall, wide, upb, tall, P(), P(), P()),
        check_vma=False)
```

```python
import jax, jax.numpy as jnp, functools
from jax import lax
from jax.experimental import pallas as pl
from jax.experimental.pallas import tpu as pltpu
from jax.sharding import Mesh, PartitionSpec as P
MESH = pl.DeviceIdType.MESH
f32 = jnp.float32
bf16 = jnp.bfloat16
EPS = 1e-05
VMEM = pl.BlockSpec(memory_space=pltpu.VMEM)

def place():
    return tuple(lax.axis_index(n) for n in ("z", "x", "core", "y"))

def chips():
    return lax.axis_size("z") * 4

def gather_kernel(count, y_first, *refs):
    n = len(y_first)
    ins, outs = refs[:n], refs[n+1:2*n+1]
    bias_in, bias_out = refs[n], refs[2*n+1]
    up_sem, down_sem, side_sem, mate_sem, recv_sem, own_send, own_recv, copy_sem, bias_sem = refs[2*n+2:]
    z, x, core, y = place()
    rows = count // 4
    quad = 2 * z + x
    dp = 2 * quad + core
    head = core == y
    sibling = (z, x, 1 - core, y)
    side = (z, 1 - x, core, y)
    above = (z + 1, x, core, y)
    below = (z - 1, x, core, y)
    mate = (z, x, core, 1 - y)
    has_up = z + 1 < rows
    has_down = z > 0
    bar = pltpu.get_barrier_semaphore()
    def sig(dev): pl.semaphore_signal(bar, inc=1, device_id=dev, device_id_type=MESH)
    sig(side)
    @pl.when(has_up)
    def _(): sig(above)
    @pl.when(has_down)
    def _(): sig(below)
    @pl.when(head)
    def _(): sig(sibling)
    @pl.when(jnp.logical_not(head))
    def _(): sig(mate)
    pl.semaphore_wait(bar, 2 + has_up.astype(jnp.int32) + has_down.astype(jnp.int32))

    def piece(m, q, sem, dev):
        part = outs[m].at[pl.ds(2 * q, 2)]
        return pltpu.make_async_remote_copy(part, part, sem.at[m, q], recv_sem.at[m, q], device_id=dev, device_id_type=MESH)

    bias_copy = pltpu.make_async_remote_copy(bias_in, bias_out, bias_sem.at[0], bias_sem.at[1], device_id=mate, device_id_type=MESH)
    @pl.when(head)
    def _():
        bias_copy.start()
        bias_out[...] = bias_in[...]
    @pl.when(jnp.logical_not(head))
    def _():
        for m in range(n):
            pltpu.make_async_remote_copy(ins[m], outs[m].at[dp], own_send.at[m], own_recv.at[m], device_id=sibling, device_id_type=MESH).start()
    def spread(m, q, up, down, across, to_mate):
        @pl.when(up)
        def _(): piece(m, q, up_sem, above).start()
        @pl.when(down)
        def _(): piece(m, q, down_sem, below).start()
        if across: piece(m, q, side_sem, side).start()
        if to_mate: piece(m, q, mate_sem, mate).start()
    def arrive(m, q): piece(m, q, up_sem, above).wait_recv()

    @pl.when(head)
    def _():
        for m in range(n):
            pltpu.make_async_copy(ins[m], outs[m].at[dp], copy_sem.at[m]).start()
        for m in range(n):
            pltpu.make_async_copy(ins[m], outs[m].at[dp], copy_sem.at[m]).wait()
            pltpu.make_async_remote_copy(ins[m], outs[m].at[dp + 1 - 2 * core], own_send.at[m], own_recv.at[m], device_id=sibling, device_id_type=MESH).wait_recv()
            spread(m, quad, has_up, has_down, True, True)

    def line(ms, last):
        def step(k, _):
            for m in ms:
                @pl.when(z - k >= 0)
                def _():
                    q = quad - 2 * k
                    arrive(m, q)
                    spread(m, q, has_up, False, True, last)
                @pl.when(z + k < rows)
                def _():
                    q = quad + 2 * k
                    arrive(m, q)
                    spread(m, q, False, has_down, True, last)
                if last:
                    @pl.when(z - k + 1 >= 0)
                    def _():
                        q = side_quad - 2 * (k - 1)
                        arrive(m, q)
                        spread(m, q, False, False, False, True)
                    @pl.when((z + k - 1 < rows) & (k > 1))
                    def _():
                        q = side_quad + 2 * (k - 1)
                        arrive(m, q)
                        spread(m, q, False, False, False, True)
            return 0
        lax.fori_loop(1, rows + (1 if last else 0), step, 0)
    side_quad = quad + 1 - 2 * x
    first = [m for m in range(n) if y_first[m]]
    later = [m for m in range(n) if not y_first[m]]
    @pl.when(head)
    def _():
        line(first, False)
        line(later, True)
    @pl.when(jnp.logical_not(head))
    def _():
        for m in first:
            arrive(m, quad)
            spread(m, quad, has_up, has_down, True, False)
        line(first, False)
        def step(q, _):
            for m in later: arrive(m, q)
            return 0
        lax.fori_loop(0, count // 2, step, 0)
    def step(k, _):
        for m in first: arrive(m, 2 * k + 1 - x)
        return 0
    lax.fori_loop(0, rows, step, 0)
    @pl.when(head)
    def _(): bias_copy.wait_send()
    @pl.when(jnp.logical_not(head))
    def _(): bias_copy.wait_recv()
    def step(k, _):
        for m in range(n):
            fam = head if not y_first[m] else True
            @pl.when(fam & (k <= z) & has_up)
            def _(): piece(m, 2 * k + x, up_sem, above).wait_send()
            @pl.when(fam & (k >= z) & has_down)
            def _(): piece(m, 2 * k + x, down_sem, below).wait_send()
            @pl.when(fam)
            def _(): piece(m, 2 * k + x, side_sem, side).wait_send()
            if not y_first[m]:
                @pl.when(head)
                def _():
                    piece(m, 2 * k, mate_sem, mate).wait_send()
                    piece(m, 2 * k + 1, mate_sem, mate).wait_send()
            else:
                @pl.when(head & (k == z))
                def _(): piece(m, quad, mate_sem, mate).wait_send()
        return 0
    lax.fori_loop(0, rows, step, 0)
    @pl.when(jnp.logical_not(head))
    def _():
        for m in range(n):
            pltpu.make_async_remote_copy(ins[m], outs[m].at[dp], own_send.at[m], own_recv.at[m], device_id=sibling, device_id_type=MESH).wait_send()

def gather(shards, bias, y_first, cid):
    count = chips()
    n = len(shards)
    dma = pltpu.SemaphoreType.DMA
    return pl.pallas_call(
        functools.partial(gather_kernel, count, y_first),
        out_shape=[jax.ShapeDtypeStruct((count,) + s.shape, s.dtype) for s in shards] + [jax.ShapeDtypeStruct(bias.shape, f32)],
        in_specs=[VMEM] * (n + 1),
        out_specs=[pl.BlockSpec(memory_space=pl.ANY)] * n + [VMEM],
        scratch_shapes=[dma((n, count // 2))] * 5 + [dma((n,))] * 3 + [dma((2,))],
        compiler_params=pltpu.CompilerParams(collective_id=cid, has_side_effects=True),
    )(*shards, bias)

def rcopy(src, dst, send, recv, dev):
    return pltpu.make_async_remote_copy(src, dst, send, recv, device_id=dev, device_id_type=MESH)

def ready(devs):
    bar = pltpu.get_barrier_semaphore()
    for dev, ok in devs:
        if ok is True:
            pl.semaphore_signal(bar, inc=1, device_id=dev, device_id_type=MESH)
        else:
            @pl.when(ok)
            def _(): pl.semaphore_signal(bar, inc=1, device_id=dev, device_id_type=MESH)
    return bar

def as_int(v): return v.astype(jnp.int32)

def halo_kernel(count, a_ref, win, sib_s, mate_s, far_s, recv, own_s):
    z, x, core, y = place()
    quad, quads = 2 * z + x, count // 2
    at_quad = lambda q: (q // 2, lax.rem(q, 2), core, y)
    sibling, mate = (z, x, 1 - core, y), (z, x, core, 1 - y)
    is1 = core == 1
    target, source = at_quad(quad - 1 + 2 * core), at_quad(quad + 1 - 2 * core)
    has_target = jnp.where(is1, quad + 1 < quads, quad > 0)
    has_source = jnp.where(is1, quad > 0, quad + 1 < quads)
    bar = ready([(sibling, True), (mate, True), (source, has_source)])
    own = 2 + 2 * core
    from_mate = 2 * core + 3 - 2 * y
    far = 6 - 6 * core
    passes = (core == y) & has_source
    extra = 5 - 4 * core
    takes = (core != y) & has_source
    @pl.when(quad == 0)
    def _():
        win[0] = jnp.zeros_like(win[0])
        @pl.when(y == 0)
        def _(): win[1] = jnp.zeros_like(win[1])
    @pl.when(quad == quads - 1)
    def _():
        win[6] = jnp.zeros_like(win[6])
        @pl.when(y == 1)
        def _(): win[5] = jnp.zeros_like(win[5])
    pl.semaphore_wait(bar, 2 + as_int(has_target))
    to_far = rcopy(a_ref, win.at[far], far_s.at[0], recv.at[far], target)
    to_mate = rcopy(a_ref, win.at[2 * core + 1 + 2 * y], mate_s.at[0], recv.at[2 * core + 1 + 2 * y], mate)
    to_sib = rcopy(a_ref, win.at[own], sib_s.at[own], recv.at[own], sibling)
    on = lambda w: rcopy(win.at[w], win.at[w], sib_s.at[w], recv.at[w], sibling)
    hand = rcopy(win.at[far], win.at[extra], mate_s.at[1], recv.at[extra], mate)
    @pl.when(has_target)
    def _(): to_far.start()
    to_mate.start()
    to_sib.start()
    win[own] = a_ref[...]
    on(from_mate).wait_recv()
    on(from_mate).start()
    @pl.when(has_source)
    def _():
        on(far).wait_recv()
        @pl.when(passes)
        def _(): hand.start()
        on(far).start()
    @pl.when(takes)
    def _():
        on(extra).wait_recv()
        on(extra).start()
    oc = 1 - core
    on(2 + 2 * oc).wait_recv()
    on(2 * oc + 3 - 2 * y).wait_recv()
    sib_source = jnp.where(is1, quad + 1 < quads, quad > 0)
    @pl.when(sib_source)
    def _():
        on(6 - 6 * oc).wait_recv()
    @pl.when(sib_source & (oc != y))
    def _(): on(5 - 4 * oc).wait_recv()
    @pl.when(has_target)
    def _(): to_far.wait_send()
    to_mate.wait_send()
    to_sib.wait_send()
    on(from_mate).wait_send()
    @pl.when(has_source)
    def _(): on(far).wait_send()
    @pl.when(passes)
    def _(): hand.wait_send()
    @pl.when(takes)
    def _(): on(extra).wait_send()

def halo(a, cid):
    count = chips()
    dma = pltpu.SemaphoreType.DMA
    return pl.pallas_call(
        functools.partial(halo_kernel, count),
        out_shape=jax.ShapeDtypeStruct((7,) + a.shape, a.dtype),
        in_specs=[VMEM], out_specs=VMEM,
        scratch_shapes=[dma((7,)), dma((2,)), dma((1,)), dma((7,)), dma((1,))],
        compiler_params=pltpu.CompilerParams(collective_id=cid, has_side_effects=True, vmem_limit_bytes=60 << 20),
    )(a)

def halo_back_kernel(count, p, out, sib_in, mate_in, far_in, stage, sib_s, sib_r, mate_s, mate_r, far_s, far_r):
    z, x, core, y = place()
    quad, quads = 2 * z + x, count // 2
    at_quad = lambda q: (q // 2, lax.rem(q, 2), core, y)
    sibling, mate = (z, x, 1 - core, y), (z, x, core, 1 - y)
    is1 = core == 1
    source, target = at_quad(quad - 1 + 2 * core), at_quad(quad + 1 - 2 * core)
    has_source = jnp.where(is1, quad + 1 < quads, quad > 0)
    has_target = jnp.where(is1, quad > 0, quad + 1 < quads)
    bar = ready([(sibling, True), (mate, True), (source, has_source)])
    pl.semaphore_wait(bar, 2 + as_int(has_target))
    own = 2 + 2 * core
    to_sib = lambda w: rcopy(p.at[w], sib_in.at[w], sib_s.at[w], sib_r.at[w], sibling)
    oc = 1 - core
    direct = lambda c: 2 * c + 3 - 2 * y
    far = lambda c: 6 - 6 * c
    extra = lambda c: 5 - 4 * c
    gives = (core != y) & has_target
    gets = (core == y) & has_target
    sib_has = has_source
    @pl.when(sib_has & (oc != y))
    def _(): to_sib(extra(oc)).start()
    to_sib(direct(oc)).start()
    @pl.when(sib_has)
    def _(): to_sib(far(oc)).start()
    to_sib(2 + 2 * oc).start()
    hand = rcopy(stage.at[0], mate_in.at[0], mate_s.at[0], mate_r.at[0], mate)
    to_mate = rcopy(stage.at[1], mate_in.at[1], mate_s.at[1], mate_r.at[1], mate)
    to_far = rcopy(stage.at[2], far_in, far_s.at[0], far_r.at[0], target)
    both = lambda w: p[w].astype(f32) + sib_in[w].astype(f32)
    @pl.when(gives)
    def _():
        to_sib(extra(core)).wait_recv()
        stage[0] = both(extra(core)).astype(bf16)
        hand.start()
    to_sib(direct(core)).wait_recv()
    stage[1] = both(direct(core)).astype(bf16)
    to_mate.start()
    @pl.when(has_target)
    def _():
        to_sib(far(core)).wait_recv()
        @pl.when(gets)
        def _():
            hand.wait_recv()
            stage[2] = (both(far(core)) + mate_in[0].astype(f32)).astype(bf16)
        @pl.when(core != y)
        def _(): stage[2] = both(far(core)).astype(bf16)
        to_far.start()
    to_sib(own).wait_recv()
    to_mate.wait_recv()
    out[...] = both(own) + mate_in[1].astype(f32)
    @pl.when(has_source)
    def _():
        to_far.wait_recv()
        out[...] = out[...] + far_in[...].astype(f32)
    @pl.when(sib_has & (oc != y))
    def _(): to_sib(extra(oc)).wait_send()
    to_sib(direct(oc)).wait_send()
    @pl.when(sib_has)
    def _(): to_sib(far(oc)).wait_send()
    to_sib(2 + 2 * oc).wait_send()
    @pl.when(gives)
    def _(): hand.wait_send()
    to_mate.wait_send()
    @pl.when(has_target)
    def _(): to_far.wait_send()

def halo_back(p, cid):
    count = chips()
    dma = pltpu.SemaphoreType.DMA
    one = p.shape[1:]
    return pl.pallas_call(
        functools.partial(halo_back_kernel, count),
        out_shape=jax.ShapeDtypeStruct(one, f32),
        in_specs=[VMEM], out_specs=VMEM,
        scratch_shapes=[pltpu.VMEM((7,) + one, bf16), pltpu.VMEM((2,) + one, bf16), pltpu.VMEM(one, bf16), pltpu.VMEM((3,) + one, bf16),
                        dma((7,)), dma((7,)), dma((2,)), dma((2,)), dma((1,)), dma((1,))],
        compiler_params=pltpu.CompilerParams(collective_id=cid, has_side_effects=True, vmem_limit_bytes=60 << 20),
    )(p)

def pair_gather_kernel(a_ref, out, send, recv):
    z, x, core, y = place()
    sibling = (z, x, 1 - core, y)
    pl.semaphore_wait(ready([(sibling, True)]), 1)
    copy = rcopy(a_ref, out.at[core], send, recv, sibling)
    copy.start()
    out[core] = a_ref[...]
    copy.wait()

def pair_gather(a, cid):
    return pl.pallas_call(
        pair_gather_kernel, out_shape=jax.ShapeDtypeStruct((2,) + a.shape, a.dtype), in_specs=[VMEM], out_specs=VMEM,
        scratch_shapes=[pltpu.SemaphoreType.DMA, pltpu.SemaphoreType.DMA],
        compiler_params=pltpu.CompilerParams(collective_id=cid, has_side_effects=True),
    )(a)

def pair_sum_kernel(p_ref, out, got, send, recv):
    z, x, core, y = place()
    sibling = (z, x, 1 - core, y)
    pl.semaphore_wait(ready([(sibling, True)]), 1)
    copy = rcopy(p_ref.at[1 - core], got, send, recv, sibling)
    copy.start()
    copy.wait()
    out[...] = p_ref[core].astype(f32) + got[...].astype(f32)

def pair_sum(p, cid):
    return pl.pallas_call(
        pair_sum_kernel, out_shape=jax.ShapeDtypeStruct(p.shape[1:], f32), in_specs=[VMEM], out_specs=VMEM,
        scratch_shapes=[pltpu.VMEM(p.shape[1:], p.dtype), pltpu.SemaphoreType.DMA, pltpu.SemaphoreType.DMA],
        compiler_params=pltpu.CompilerParams(collective_id=cid, has_side_effects=True),
    )(p)


def small_sum_kernel(rows, layers, *refs):
    per = 9
    ins, refs = refs[:layers * per], refs[layers * per:]
    gains, shifts, obias, qvb, upb, v, got, acc, zin, send, recv, z_s, z_r = refs
    z, x, core, y = place()
    width, half = v.shape[1], v.shape[1] // 2
    spans_up = ins[per - 1].shape[1] // width
    stride = 8 + 2 * spans_up
    peers = [(z, x, 1 - core, y), (z, 1 - x, core, y), (z, x, core, 1 - y)]
    others = [lax.rem(z + d, rows) for d in range(1, rows)]
    at = lambda o: (o, x, core, y)
    bar = ready([(p, True) for p in peers] + [(at(o), True) for o in others])
    v[...] = jnp.zeros_like(v)
    for l in range(layers):
        one, b = ins[l * per:(l + 1) * per], l * stride
        for i in range(6): v[b + i:b + i + 1, :] = one[i][...]
        for c in range(2):
            @pl.when(core == c)
            def _():
                for i in range(2): v[b + 6 + i:b + 7 + i, c * half:(c + 1) * half] = one[6 + i][...]
                for i in range(spans_up):
                    r = b + 8 + c * spans_up + i
                    v[r:r + 1, :] = one[8][:, i * width:(i + 1) * width]
    pl.semaphore_wait(bar, 3 + rows - 1)
    src = v
    for i, p in enumerate(peers):
        copy = rcopy(src, got.at[i], send.at[i], recv.at[i], p)
        copy.start()
        copy.wait()
        acc[i] = src[...] + got[i]
        src = acc.at[i]
    to = lambda o, slot: rcopy(src, zin.at[slot], z_s.at[o], z_r.at[slot], at(o))
    for o in others: to(o, z).start()
    zin[z] = src[...]
    for o in others: to(o, o).wait_recv()
    total = zin[0]
    for i in range(1, rows): total = total + zin[i]
    v[...] = total
    for l in range(layers):
        b = l * stride
        for i in range(2):
            gains[l, i:i + 1, :] = v[b + i:b + i + 1, :]
            shifts[l, i:i + 1, :] = v[b + 2 + i:b + 3 + i, :]
            obias[l, i:i + 1, :] = v[b + 4 + i:b + 5 + i, :]
        for c in range(2):
            @pl.when(y == c)
            def _():
                for i in range(2): qvb[l, i:i + 1, :] = v[b + 6 + i:b + 7 + i, c * half:(c + 1) * half]
                for i in range(spans_up):
                    r = b + 8 + c * spans_up + i
                    upb[l:l + 1, i * width:(i + 1) * width] = v[r:r + 1, :]
    for o in others: to(o, z).wait_send()

def small_sum(parts, cid):
    rows = lax.axis_size("z")
    dma = pltpu.SemaphoreType.DMA
    layers, width, hidden = len(parts), parts[0][0].shape[1], parts[0][8].shape[1]
    flat = [t for p in parts for t in p]
    one = (layers * (8 + 2 * hidden // width), width)
    pair = jax.ShapeDtypeStruct((layers, 2, width), f32)
    return pl.pallas_call(
        functools.partial(small_sum_kernel, rows, layers),
        out_shape=[pair, pair, pair, jax.ShapeDtypeStruct((layers, 2, width // 2), f32), jax.ShapeDtypeStruct((layers, hidden), f32)],
        in_specs=[VMEM] * len(flat), out_specs=[VMEM] * 5,
        scratch_shapes=[pltpu.VMEM(one, f32), pltpu.VMEM((3,) + one, f32), pltpu.VMEM((3,) + one, f32), pltpu.VMEM((rows,) + one, f32),
                        dma((3,)), dma((3,)), dma((rows,)), dma((rows,))],
        compiler_params=pltpu.CompilerParams(collective_id=cid, has_side_effects=True, vmem_limit_bytes=60 << 20),
    )(*flat)

def reduce_kernel(count, early, *refs):
    n = len(early)
    rows = count // 4
    grads, outs = refs[:n], refs[n:2*n]
    k = 2*n
    mate_in, side_out, side_in, line_out, up_in, down_in, final_out = [refs[k+i*n:k+(i+1)*n] for i in range(7)]
    k += 7*n
    (mate_s, mate_r, side_s, side_r, up_s, up_r, down_s, down_r, last_s, last_r) = refs[k:]
    z, x, core, y = place()
    quad = 2 * z + x
    dp = 2 * quad + core
    head = core == y
    other = jnp.logical_not(head)
    sibling = (z, x, 1 - core, y)
    side = (z, 1 - x, core, y)
    above = (z + 1, x, core, y)
    below = (z - 1, x, core, y)
    mate = (z, x, core, 1 - y)
    has_up = z + 1 < rows
    has_down = z > 0
    for m in range(n):
        @pl.when(z == 0)
        def _(): up_in[m][...] = jnp.zeros_like(up_in[m])
        @pl.when(z == rows - 1)
        def _(): down_in[m][...] = jnp.zeros_like(down_in[m])
    bar = pltpu.get_barrier_semaphore()
    def sig(dev): pl.semaphore_signal(bar, inc=1, device_id=dev, device_id_type=MESH)
    sig(side)
    @pl.when(has_up)
    def _(): sig(above)
    @pl.when(has_down)
    def _(): sig(below)
    @pl.when(head)
    def _(): sig(mate)
    @pl.when(other)
    def _(): sig(sibling)
    pl.semaphore_wait(bar, 2 + has_up.astype(jnp.int32) + has_down.astype(jnp.int32))

    def rc(src, dst, s, r, dev):
        return pltpu.make_async_remote_copy(src, dst, s, r, device_id=dev, device_id_type=MESH)
    def to_mate(m, q):
        return rc(grads[m].at[pl.ds(2*q, 2)], mate_in[m].at[pl.ds(2*q, 2)], mate_s.at[m, q], mate_r.at[m, q], mate)
    def to_side(m, j):
        return rc(side_out[m].at[j], side_in[m].at[j], side_s.at[m, j], side_r.at[m, j], side)
    def to_up(m, j):
        return rc(line_out[m].at[j], up_in[m].at[j], up_s.at[m, j], up_r.at[m, j], above)
    def to_down(m, j):
        return rc(line_out[m].at[j], down_in[m].at[j], down_s.at[m, j], down_r.at[m, j], below)
    def late_mate(m):
        return rc(line_out[m].at[z], mate_in[m], mate_s.at[m, quad], mate_r.at[m, quad], mate)
    def last(m):
        return rc(final_out[m], outs[m], last_s.at[m], last_r.at[m], sibling)

    def far_first(fn):
        def step(i, _):
            d = rows - i
            for j, ok in ((z + d, z + d < rows), (z - d, z - d >= 0)):
                @pl.when(ok)
                def _(): fn(j)
            return 0
        lax.fori_loop(1, rows, step, 0)
        fn(z)

    order = [m for m in range(n) if early[m]], [m for m in range(n) if not early[m]]

    @pl.when(other)
    def _():
        def go(j):
            for m in order[0]:
                to_mate(m, 2 * j + 1 - x).start()
        def go2(j):
            for m in order[0]:
                to_mate(m, 2 * j + x).start()
        far_first(go); far_first(go2)

    def own(m, q, c, with_mate):
        t = grads[m][2*q+c].astype(f32)
        return t + mate_in[m][2*q+c].astype(f32) if with_mate else t

    def side_stage(ms, with_mate):
        def go(j):
            q = 2 * j + 1 - x
            for m in ms:
                if with_mate: to_mate(m, q).wait_recv()
                def half(c, _):
                    side_out[m][j, c] = own(m, q, c, with_mate).astype(bf16)
                    return 0
                lax.fori_loop(0, 2, half, 0)
            for m in ms:
                to_side(m, j).start()
        far_first(go)

    def line_stage(ms, with_mate):
        def go(j):
            q = 2 * j + x
            for m in ms:
                if with_mate: to_mate(m, q).wait_recv()
                to_side(m, j).wait_recv()
                @pl.when((j >= z) & has_down)
                def _(): to_up(m, j).wait_recv()
                @pl.when((j <= z) & has_up)
                def _(): to_down(m, j).wait_recv()
                def half(c, _):
                    t = own(m, q, c, with_mate) + side_in[m][j, c].astype(f32)
                    @pl.when(j > z)
                    def _(): line_out[m][j, c] = (t + up_in[m][j, c].astype(f32)).astype(bf16)
                    @pl.when(j < z)
                    def _(): line_out[m][j, c] = (t + down_in[m][j, c].astype(f32)).astype(bf16)
                    @pl.when(j == z)
                    def _():
                        u = t + up_in[m][j, c].astype(f32) + down_in[m][j, c].astype(f32)
                        if with_mate:
                            @pl.when(c == core)
                            def _(): outs[m][...] = u
                            @pl.when(c != core)
                            def _(): final_out[m][...] = u
                        else:
                            @pl.when(other)
                            def _(): line_out[m][j, c] = u.astype(bf16)
                            @pl.when(head & (c == core))
                            def _(): outs[m][...] = u
                            @pl.when(head & (c != core))
                            def _(): final_out[m][...] = u
                    return 0
                lax.fori_loop(0, 2, half, 0)
            for m in ms:
                @pl.when(j > z)
                def _(): to_up(m, j).start()
                @pl.when(j < z)
                def _(): to_down(m, j).start()
        far_first(go)

    side_stage(order[1], False)
    @pl.when(head)
    def _(): side_stage(order[0], True)
    line_stage(order[1], False)
    @pl.when(other)
    def _():
        for m in order[1]: late_mate(m).start()
    @pl.when(head)
    def _():
        line_stage(order[0], True)
        for m in order[1]:
            late_mate(m).wait_recv()
            outs[m][...] = outs[m][...] + mate_in[m][core].astype(f32)
            final_out[m][...] = final_out[m][...] + mate_in[m][1 - core].astype(f32)
        for m in range(n):
            last(m).start()
    @pl.when(other)
    def _():
        for m in range(n): last(m).wait_recv()
    def step(j, _):
        for m in range(n):
            fam = head if early[m] else True
            @pl.when(fam)
            def _(): to_side(m, j).wait_send()
            @pl.when(fam & (j > z))
            def _(): to_up(m, j).wait_send()
            @pl.when(fam & (j < z))
            def _(): to_down(m, j).wait_send()
            if early[m]:
                @pl.when(other)
                def _():
                    to_mate(m, 2 * j).wait_send()
                    to_mate(m, 2 * j + 1).wait_send()
        return 0
    lax.fori_loop(0, rows, step, 0)
    for m in range(n):
        @pl.when(head)
        def _(): last(m).wait_send()
        if not early[m]:
            @pl.when(other)
            def _(): late_mate(m).wait_send()

def scatter_sum(grads, early, cid):
    count = chips()
    n = len(grads)
    rows = count // 4
    dma = pltpu.SemaphoreType.DMA
    quads = [pltpu.VMEM((rows, 2) + g.shape[1:], bf16) for g in grads]
    mates = [pltpu.VMEM(((count if e else 2),) + g.shape[1:], bf16) for g, e in zip(grads, early)]
    lasts = [pltpu.VMEM(g.shape[1:], f32) for g in grads]
    return pl.pallas_call(
        functools.partial(reduce_kernel, count, early),
        out_shape=[jax.ShapeDtypeStruct(g.shape[1:], f32) for g in grads],
        in_specs=[pl.BlockSpec(memory_space=pltpu.VMEM)] * n,
        out_specs=[pl.BlockSpec(memory_space=pltpu.VMEM)] * n,
        scratch_shapes=mates + quads * 5 + lasts + [dma((n, count // 2))] * 2 + [dma((n, rows))] * 6 + [dma((n,))] * 2,
        compiler_params=pltpu.CompilerParams(collective_id=cid, has_side_effects=True, vmem_limit_bytes=60 << 20),
    )(*grads)
TQ, TK, BQ, BK = 384, 512, 384, 512
NEG = -1e30

def nt(a, b):
    return lax.dot_general(a, b, (((1,), (1,)), ((), ())), preferred_element_type=f32)
def tn(a, b):
    return lax.dot_general(a, b, (((0,), (0,)), ((), ())), preferred_element_type=f32)

def fold(t, op):
    out = t[:, :128]
    for i in range(1, t.shape[1] // 128):
        out = op(out, t[:, i*128:(i+1)*128])
    return out

def tiled(t, n):
    return t if n == 128 else jnp.concatenate([t] * (n // 128), axis=1)

def tile_at(lo, j, size, wide):
    want = lo + j * size
    start = jnp.minimum(want, wide - size)
    return pl.multiple_of(start, 128), want - start

def fwd_kernel(half, span_ref, q_ref, k_ref, v_ref, idq_ref, idk_ref, o_ref, lse_ref, s_scr, m_scr, l_scr, acc):
    i = pl.program_id(0)
    T = q_ref.shape[0]
    pairs = q_ref.shape[1] // 128
    wide = k_ref.shape[0]
    lo, steps = span_ref[0, i], span_ref[1, i]
    low = lax.broadcasted_iota(jnp.int32, (T, 128), 1) < 64
    qs = []
    for p in range(pairs):
        qp = q_ref[:, p*128:(p+1)*128] * jnp.bfloat16(0.125)
        z = jnp.zeros_like(qp)
        qs += [jnp.where(low, qp, z), jnp.where(low, z, qp)]
    gap = 2 * half + i * T + jnp.where(i >= half // T, half, 0)
    idq = idq_ref[...]
    col = lax.broadcasted_iota(jnp.int32, (T, TK), 1)
    rel = col - lax.broadcasted_iota(jnp.int32, (T, TK), 0)
    for h in range(2 * pairs):
        m_scr[h] = jnp.full((T, 128), NEG, f32)
        l_scr[h] = jnp.zeros((T, 128), f32)
    for p in range(pairs):
        acc[p] = jnp.zeros((T, 128), f32)
    def scores(j, _):
        start, fresh = tile_at(lo, j, TK, wide)
        ok = ((idq == idk_ref[0:1, pl.ds(start, TK)]) | (rel == gap - start)) & (col >= fresh)
        for h in range(2 * pairs):
            p = h // 2
            s = jnp.where(ok, nt(qs[h], k_ref[pl.ds(start, TK), p*128:(p+1)*128]), NEG)
            s_scr[h, j] = s
            m_scr[h] = jnp.maximum(m_scr[h], fold(s, jnp.maximum))
        return 0
    lax.fori_loop(0, steps, scores, 0)
    for h in range(2 * pairs):
        m_scr[h] = jnp.broadcast_to(jnp.max(m_scr[h], axis=1, keepdims=True), (T, 128))
    def values(j, _):
        start, fresh = tile_at(lo, j, TK, wide)
        for p in range(pairs):
            vp = v_ref[pl.ds(start, TK), p*128:(p+1)*128]
            out = []
            for h in (2*p, 2*p+1):
                e = jnp.exp(s_scr[h, j] - tiled(m_scr[h], TK))
                l_scr[h] = l_scr[h] + fold(e, jnp.add)
                out.append(jnp.dot(e.astype(bf16), vp, preferred_element_type=f32))
            acc[p] = acc[p] + jnp.where(low, out[0], out[1])
        return 0
    lax.fori_loop(0, steps, values, 0)
    for p in range(pairs):
        inv = [1.0 / jnp.sum(l_scr[h], axis=1, keepdims=True) for h in (2*p, 2*p+1)]
        o_ref[:, p*128:(p+1)*128] = (acc[p] * jnp.where(low, inv[0], inv[1])).astype(bf16)
    for h in range(2 * pairs):
        total = jnp.sum(l_scr[h].T, axis=0, keepdims=True)
        lse_ref[h:h+1, :] = m_scr[h].T[0:1, :] + jnp.log(total)

def attend(q, k, v, span, idq, idk):
    rows, cols = q.shape
    wide = k.shape[0]
    heads = cols // 64
    tiles = rows // TQ
    full = lambda a: pl.BlockSpec(a.shape, lambda i, s: (0,) * a.ndim)
    most = (4 * (rows // 2) + TQ + TK) // TK + 1
    return pl.pallas_call(
        functools.partial(fwd_kernel, rows // 2),
        grid_spec=pltpu.PrefetchScalarGridSpec(
            num_scalar_prefetch=1, grid=(tiles,),
            in_specs=[pl.BlockSpec((TQ, cols), lambda i, s: (i, 0)), full(k), full(v),
                      pl.BlockSpec((TQ, 1), lambda i, s: (i, 0)), full(idk)],
            out_specs=[pl.BlockSpec((TQ, cols), lambda i, s: (i, 0)), pl.BlockSpec((heads, TQ), lambda i, s: (0, i))],
            scratch_shapes=[pltpu.VMEM((heads, most, TQ, TK), f32), pltpu.VMEM((heads, TQ, 128), f32), pltpu.VMEM((heads, TQ, 128), f32),
                            pltpu.VMEM((heads // 2, TQ, 128), f32)]),
        out_shape=[jax.ShapeDtypeStruct((rows, cols), bf16), jax.ShapeDtypeStruct((heads, rows), f32)],
        compiler_params=pltpu.CompilerParams(vmem_limit_bytes=60 << 20, dimension_semantics=("arbitrary",)),
        cost_estimate=pl.CostEstimate(flops=4*rows*wide*cols, bytes_accessed=6*wide*cols, transcendentals=0),
    )(span, q, k, v, idq, idk)

def bwd_kernel(half, span_ref, q_ref, k_ref, v_ref, o_ref, da_ref, lse_ref, idq_ref, idk_ref, dq_ref, dk_ref, dv_ref, dk_acc, dv_acc, dq_acc):
    i = pl.program_id(0)
    T = q_ref.shape[0]
    pairs = q_ref.shape[1] // 128
    wide = k_ref.shape[0]
    lo, steps = span_ref[0, i], span_ref[1, i]
    low = lax.broadcasted_iota(jnp.int32, (T, 128), 1) < 64
    @pl.when(i == 0)
    def _():
        dk_acc[...] = jnp.zeros_like(dk_acc)
        dv_acc[...] = jnp.zeros_like(dv_acc)
    qs, das, delta = [], [], []
    for p in range(pairs):
        at = slice(p*128, (p+1)*128)
        qp = q_ref[:, at] * jnp.bfloat16(0.125)
        dp = da_ref[:, at]
        z = jnp.zeros_like(qp)
        qs += [jnp.where(low, qp, z), jnp.where(low, z, qp)]
        das += [jnp.where(low, dp, z), jnp.where(low, z, dp)]
        t = (dp.astype(f32) * o_ref[:, at].astype(f32)).T
        delta += [jnp.sum(t[:64], axis=0, keepdims=True), jnp.sum(t[64:], axis=0, keepdims=True)]
        dq_acc[p] = jnp.zeros((T, 128), f32)
    gap = 2 * half + i * T + jnp.where(i >= half // T, half, 0)
    idq = idq_ref[...]
    row = lax.broadcasted_iota(jnp.int32, (BK, T), 0)
    rel = row - lax.broadcasted_iota(jnp.int32, (BK, T), 1)
    def tile(j, _):
        start, fresh = tile_at(lo, j, BK, wide)
        at_rows = pl.ds(start, BK)
        ok = ((idk_ref[at_rows, :] == idq) | (rel == gap - start)) & (row >= fresh)
        for p in range(pairs):
            at = slice(p*128, (p+1)*128)
            kp, vp = k_ref[at_rows, at], v_ref[at_rows, at]
            kx = kp * jnp.bfloat16(0.125)
            dk = dv = 0
            dq = []
            for h in (2*p, 2*p+1):
                s = jnp.where(ok, nt(kp, qs[h]), NEG)
                pr = jnp.exp(s - lse_ref[h:h+1, :])
                ds = (pr * (nt(vp, das[h]) - delta[h])).astype(bf16)
                dv = dv + jnp.dot(pr.astype(bf16), das[h], preferred_element_type=f32)
                dk = dk + jnp.dot(ds, qs[h], preferred_element_type=f32)
                dq.append(tn(ds, kx))
            dq_acc[p] = dq_acc[p] + jnp.where(low, dq[0], dq[1])
            dk_acc[at_rows, at] = dk_acc[at_rows, at] + dk
            dv_acc[at_rows, at] = dv_acc[at_rows, at] + dv
        return 0
    lax.fori_loop(0, steps, tile, 0)
    for p in range(pairs):
        dq_ref[:, p*128:(p+1)*128] = dq_acc[p].astype(dq_ref.dtype)
    @pl.when(i == pl.num_programs(0) - 1)
    def _():
        dk_ref[...] = dk_acc[...].astype(bf16)
        dv_ref[...] = dv_acc[...].astype(bf16)

def attend_back(q, k, v, o, da, lse, span, idq_row, idk_col):
    rows, cols = q.shape
    wide = k.shape[0]
    heads = cols // 64
    tiles = rows // BQ
    full = lambda a: pl.BlockSpec(a.shape, lambda i, s: (0,) * a.ndim)
    qt = pl.BlockSpec((BQ, cols), lambda i, s: (i, 0))
    return pl.pallas_call(
        functools.partial(bwd_kernel, rows // 2),
        grid_spec=pltpu.PrefetchScalarGridSpec(
            num_scalar_prefetch=1, grid=(tiles,),
            in_specs=[qt, full(k), full(v), qt, qt, pl.BlockSpec((heads, BQ), lambda i, s: (0, i)),
                      pl.BlockSpec((1, BQ), lambda i, s: (0, i)), full(idk_col)],
            out_specs=[qt, full(k), full(v)],
            scratch_shapes=[pltpu.VMEM((wide, cols), f32), pltpu.VMEM((wide, cols), f32), pltpu.VMEM((heads // 2, BQ, 128), f32)]),
        out_shape=[jax.ShapeDtypeStruct((rows, cols), bf16), jax.ShapeDtypeStruct((wide, cols), bf16), jax.ShapeDtypeStruct((wide, cols), bf16)],
        compiler_params=pltpu.CompilerParams(vmem_limit_bytes=60 << 20, dimension_semantics=("arbitrary",)),
        cost_estimate=pl.CostEstimate(flops=10*rows*wide*cols, bytes_accessed=10*wide*cols, transcendentals=0),
    )(span, q, k, v, o, da, lse, idq_row, idk_col)

def spans(ids, mine, tq, tk):
    first, final = mine[::tq], mine[tq-1::tq]
    lo = jnp.sum((ids[None, :] < first[:, None]).astype(jnp.int32), axis=1) // 128 * 128
    hi = jnp.sum((ids[None, :] <= final[:, None]).astype(jnp.int32), axis=1)
    return jnp.stack([lo, (hi - lo + tk - 1) // tk])

def window_ids(clip_ids, frame_mask, half):
    z, x, core, y = place()
    start = (4 * (2 * z + x) + y) * half
    pad = 4 * half
    ids = jnp.pad(clip_ids, (2 * half, pad), constant_values=((-1, 1 << 30),))
    val = jnp.pad(frame_mask, (2 * half, pad))
    ids = lax.dynamic_slice_in_dim(ids, start, 7 * half)
    val = lax.dynamic_slice_in_dim(val, start, 7 * half)
    mine = jnp.concatenate([ids[2*half:3*half], ids[4*half:5*half]])
    keys = jnp.where(val == 1, ids, -2)
    return spans(ids, mine, TQ, TK), spans(ids, mine, BQ, BK), mine, keys

def norm_forward(values, gain_vec, bias_vec):
    row_mean = jnp.mean(values, axis=-1, keepdims=True)
    centred = values - row_mean
    inverse = lax.rsqrt(jnp.mean(centred * centred, axis=-1, keepdims=True) + EPS)
    normed = centred * inverse
    return ((normed * gain_vec + bias_vec).astype(bf16), normed, inverse)

def norm_backward(grad_out, normed, inverse, gain_vec):
    scaled = grad_out * gain_vec
    projected = (scaled - jnp.mean(scaled, axis=-1, keepdims=True)
                 - normed * jnp.mean(scaled * normed, axis=-1, keepdims=True))
    return (inverse * projected, jnp.sum(grad_out * normed, axis=0, keepdims=True), jnp.sum(grad_out, axis=0, keepdims=True))

def gelu_parts(z):
    half = 0.5 * (1.0 + jax.scipy.special.erf(z * 0.7071067811865476))
    return z * half, half + z * jnp.exp(-0.5 * z * z) * 0.3989422804014327

def mm(a, b):
    return jnp.dot(a, b, preferred_element_type=f32)

def pack(parts, width):
    return jnp.concatenate([p[..., i:i + width] for p in parts for i in range(0, p.shape[-1], width)], axis=1)

def unpack(packed, shapes, width):
    out, at = [], 0
    for r, c in shapes:
        n = c // width
        out.append(jnp.concatenate([packed[:, at + i * r:at + (i + 1) * r] for i in range(n)], axis=-1))
        at += n * r
    return out

def swap(t):
    return lax.ppermute(t, ("core", "y"), [(0, 0), (1, 2), (2, 1), (3, 3)])

def body(frames_in, frames_cot, clip_ids, frame_mask, norm_gain, norm_bias, qkv_weight, qv_bias,
         proj_weight, up_weight, up_bias, down_weight, out_biases):
    layers = qkv_weight.shape[0]
    half, width = frames_in.shape
    z, x, core, y = place()
    count = chips()
    group = ("z", "x", "y")
    hcols = qkv_weight.shape[-1]
    hidden = up_weight.shape[-1]
    span, span_back, mine, keys = window_ids(clip_ids, frame_mask, half)
    idk = keys[None, :]
    shards = [[qkv_weight[l].reshape(-1, 3 * hcols), proj_weight[l], up_weight[l], down_weight[l]] for l in range(layers)]
    bias = jnp.concatenate([up_bias, qv_bias.reshape(layers, 2 * hcols)], axis=1)
    halves = lambda t: t.reshape(-1, width)
    soon = [shards[0][1], shards[0][3], halves(shards[1][0])]
    late = shards[1][1:]
    moved = swap(pack([t[None] for t in soon], width)[0])
    moved_late = swap(pack([t[None] for t in late], width)[0])
    wqkv0, wup0, bias = gather([shards[0][0], shards[0][2]], bias, [False, True], 0)
    moved, wqkv0, wup0 = lax.optimization_barrier((moved, wqkv0, wup0))
    every = lambda t: lax.all_gather(t, group, axis=0, tiled=False)
    rows_of = lambda w: w.reshape(-1, w.shape[-1])
    got = every(moved)
    full = [[rows_of(wqkv0), None, rows_of(wup0), None], None]
    state = frames_in
    kept = []
    for l in range(layers):
        wqkv = full[l][0]
        upb, qb, vb = bias[l, :hidden], bias[l, hidden:hidden+hcols], bias[l, hidden+hcols:]
        a, hat1, inv1 = norm_forward(state, norm_gain[l, 0], norm_bias[l, 0])
        win = halo(a, 1)
        a_own = jnp.concatenate([win[2], win[4]])
        a_win = win.reshape(-1, width)
        q = (mm(a_own, wqkv[:, :hcols]) + qb).astype(bf16)
        k = mm(a_win, wqkv[:, hcols:2*hcols]).astype(bf16)
        v = (mm(a_win, wqkv[:, 2*hcols:]) + vb).astype(bf16)
        o, lse = attend(q, k, v, span, mine[:, None], idk)
        o, got = lax.optimization_barrier((o, got))
        if l == 0:
            wproj, wdown, nxt = [rows_of(w) for w in unpack(got, [t.shape for t in soon], width)]
            full = [[full[0][0], wproj, full[0][2], wdown], [nxt.reshape(-1, 3 * hcols)]]
            moved_late, wproj = lax.optimization_barrier((moved_late, wproj))
            full[0][1] = wproj
            got = every(moved_late)
        else:
            full[1] += [rows_of(w) for w in unpack(got, [t.shape for t in late], width)]
        wqkv, wproj, wup, wdown = full[l]
        middle = state + pair_sum(mm(o, wproj).astype(bf16).reshape(2, half, width), 2) + out_biases[l, 0]
        c, hat2, inv2 = norm_forward(middle, norm_gain[l, 1], norm_bias[l, 1])
        c_full = pair_gather(c, 3).reshape(2 * half, width)
        zz = mm(c_full, wup) + upb
        g, slope = gelu_parts(zz)
        g, slope = g.astype(bf16), slope.astype(bf16)
        state = middle + pair_sum(mm(g, wdown).astype(bf16).reshape(2, half, width), 2) + out_biases[l, 1]
        kept.append((a_own, a_win, hat1, inv1, q, k, v, o, lse, hat2, inv2, c_full, g, slope))
    grad = frames_cot
    wgrads, small = [None] * layers, [None] * layers
    for l in reversed(range(layers)):
        wqkv, wproj, wup, wdown = full[l]
        a_own, a_win, hat1, inv1, q, k, v, o, lse, hat2, inv2, c_full, g, slope = kept[l]
        e_full = pair_gather(grad.astype(bf16), 3).reshape(2 * half, width)
        g_down = mm(g.T, e_full)
        dz = mm(e_full, wdown.T) * slope.astype(f32)
        upb = jnp.sum(dz, axis=0, keepdims=True)
        dzb = dz.astype(bf16)
        g_up = mm(c_full.T, dzb)
        dc = pair_sum(mm(dzb, wup.T).astype(bf16).reshape(2, half, width), 2)
        back, gain2, shift2 = norm_backward(dc, hat2, inv2, norm_gain[l, 1])
        dh = grad + back
        dh_full = pair_gather(dh.astype(bf16), 3).reshape(2 * half, width)
        g_proj = mm(o.T, dh_full)
        da = mm(dh_full, wproj.T).astype(bf16)
        dq, dk, dv = attend_back(q, k, v, o, da, lse, span_back, mine[None, :], keys[:, None])
        qb = jnp.sum(dq.astype(f32), axis=0, keepdims=True)
        vb = jnp.sum(dv.astype(f32), axis=0, keepdims=True)
        g_qkv = jnp.concatenate([mm(a_own.T, dq), mm(a_win.T, dk), mm(a_win.T, dv)], axis=1)
        wq, wk, wv = wqkv[:, :hcols], wqkv[:, hcols:2*hcols], wqkv[:, 2*hcols:]
        part = mm(dk, wk.T) + mm(dv, wv.T)
        part = part.reshape(7, half, width)
        pq = mm(dq, wq.T).reshape(2, half, width)
        part = jnp.stack([part[0], part[1], part[2] + pq[0], part[3], part[4] + pq[1], part[5], part[6]]).astype(bf16)
        da1 = halo_back(part, 4)
        back, gain1, shift1 = norm_backward(da1, hat1, inv1, norm_gain[l, 0])
        small[l] = [gain1, gain2, shift1, shift2, jnp.sum(dh, axis=0, keepdims=True), jnp.sum(grad, axis=0, keepdims=True), qb, vb, upb]
        grad = dh + back
        grads = [t.astype(bf16).reshape(count, -1, t.shape[-1]) for t in (g_qkv, g_proj, g_up, g_down)]
        if l == 0:
            own, grads[0] = lax.optimization_barrier((own, grads[0]))
            wgrads[1] = [w[0] for w in unpack(swap(own)[None].astype(f32), [s.shape for s in shards[1]], hcols)]
            wgrads[l] = scatter_sum(grads, [False, True, False, True], 5)
        else:
            packed = pack(grads, hcols)
            packed, grad = lax.optimization_barrier((packed, grad))
            rows = packed.shape[1]
            own = lax.psum_scatter(packed.reshape(-1, hcols), group, scatter_dimension=0, tiled=True)
    gains, shifts, obias, qvb, upb = small_sum(small, 6)
    gq, gp, gu, gd = [jnp.stack([w[i] for w in wgrads]) for i in range(4)]
    return (state, grad, gq.reshape(layers, -1, 3, hcols), qvb, gp, gu, upb, gd, gains, shifts, obias)

def solution(mesh):
    dp, mp = mesh.shape["dp"], mesh.shape["mp"]
    named = Mesh(mesh.devices.reshape(dp // 4, 2, 2, mp), ("z", "x", "core", "y"))
    deep = ("z", "x", "core")
    rows = P(deep + ("y",), None)
    qkv, qv = P(None, deep, None, "y"), P(None, None, "y")
    tall, wide, upb = P(None, ("y",) + deep, None), P(None, deep, "y"), P(None, "y")
    return jax.shard_map(
        body, mesh=named,
        in_specs=(rows, rows, P(), P(), P(), P(), qkv, qv, tall, wide, upb, tall, P()),
        out_specs=(rows, rows, qkv, qv, tall, wide, upb, tall, P(), P(), P()),
        check_vma=False)
```

```python
import jax, jax.numpy as jnp, functools
from jax import lax
from jax.experimental import pallas as pl
from jax.experimental.pallas import tpu as pltpu
from jax.sharding import Mesh, PartitionSpec as P
MESH = pl.DeviceIdType.MESH
f32 = jnp.float32
bf16 = jnp.bfloat16
EPS = 1e-05
VMEM = pl.BlockSpec(memory_space=pltpu.VMEM)

def place():
    return tuple(lax.axis_index(n) for n in ("z", "x", "core", "y"))

def chips():
    return lax.axis_size("z") * 4

def gather_kernel(count, y_first, *refs):
    n = len(y_first)
    ins, outs = refs[:n], refs[n+1:2*n+1]
    bias_in, bias_out = refs[n], refs[2*n+1]
    up_sem, down_sem, side_sem, mate_sem, recv_sem, own_send, own_recv, copy_sem, bias_sem = refs[2*n+2:]
    z, x, core, y = place()
    rows = count // 4
    quad = 2 * z + x
    dp = 2 * quad + core
    head = core == y
    sibling = (z, x, 1 - core, y)
    side = (z, 1 - x, core, y)
    above = (z + 1, x, core, y)
    below = (z - 1, x, core, y)
    mate = (z, x, core, 1 - y)
    has_up = z + 1 < rows
    has_down = z > 0
    bar = pltpu.get_barrier_semaphore()
    def sig(dev): pl.semaphore_signal(bar, inc=1, device_id=dev, device_id_type=MESH)
    sig(side)
    @pl.when(has_up)
    def _(): sig(above)
    @pl.when(has_down)
    def _(): sig(below)
    @pl.when(head)
    def _(): sig(sibling)
    @pl.when(jnp.logical_not(head))
    def _(): sig(mate)
    pl.semaphore_wait(bar, 2 + has_up.astype(jnp.int32) + has_down.astype(jnp.int32))

    def piece(m, q, sem, dev):
        part = outs[m].at[pl.ds(2 * q, 2)]
        return pltpu.make_async_remote_copy(part, part, sem.at[m, q], recv_sem.at[m, q], device_id=dev, device_id_type=MESH)

    bias_copy = pltpu.make_async_remote_copy(bias_in, bias_out, bias_sem.at[0], bias_sem.at[1], device_id=mate, device_id_type=MESH)
    @pl.when(head)
    def _():
        bias_copy.start()
        bias_out[...] = bias_in[...]
    @pl.when(jnp.logical_not(head))
    def _():
        for m in range(n):
            pltpu.make_async_remote_copy(ins[m], outs[m].at[dp], own_send.at[m], own_recv.at[m], device_id=sibling, device_id_type=MESH).start()
    def spread(m, q, up, down, across, to_mate):
        @pl.when(up)
        def _(): piece(m, q, up_sem, above).start()
        @pl.when(down)
        def _(): piece(m, q, down_sem, below).start()
        if across: piece(m, q, side_sem, side).start()
        if to_mate: piece(m, q, mate_sem, mate).start()
    def arrive(m, q): piece(m, q, up_sem, above).wait_recv()

    @pl.when(head)
    def _():
        for m in range(n):
            pltpu.make_async_copy(ins[m], outs[m].at[dp], copy_sem.at[m]).start()
        for m in range(n):
            pltpu.make_async_copy(ins[m], outs[m].at[dp], copy_sem.at[m]).wait()
            pltpu.make_async_remote_copy(ins[m], outs[m].at[dp + 1 - 2 * core], own_send.at[m], own_recv.at[m], device_id=sibling, device_id_type=MESH).wait_recv()
            spread(m, quad, has_up, has_down, True, True)

    def line(ms, last):
        def step(k, _):
            for m in ms:
                @pl.when(z - k >= 0)
                def _():
                    q = quad - 2 * k
                    arrive(m, q)
                    spread(m, q, has_up, False, True, last)
                @pl.when(z + k < rows)
                def _():
                    q = quad + 2 * k
                    arrive(m, q)
                    spread(m, q, False, has_down, True, last)
                if last:
                    @pl.when(z - k + 1 >= 0)
                    def _():
                        q = side_quad - 2 * (k - 1)
                        arrive(m, q)
                        spread(m, q, False, False, False, True)
                    @pl.when((z + k - 1 < rows) & (k > 1))
                    def _():
                        q = side_quad + 2 * (k - 1)
                        arrive(m, q)
                        spread(m, q, False, False, False, True)
            return 0
        lax.fori_loop(1, rows + (1 if last else 0), step, 0)
    side_quad = quad + 1 - 2 * x
    first = [m for m in range(n) if y_first[m]]
    later = [m for m in range(n) if not y_first[m]]
    @pl.when(head)
    def _():
        line(first, False)
        line(later, True)
    @pl.when(jnp.logical_not(head))
    def _():
        for m in first:
            arrive(m, quad)
            spread(m, quad, has_up, has_down, True, False)
        line(first, False)
        def step(q, _):
            for m in later: arrive(m, q)
            return 0
        lax.fori_loop(0, count // 2, step, 0)
    def step(k, _):
        for m in first: arrive(m, 2 * k + 1 - x)
        return 0
    lax.fori_loop(0, rows, step, 0)
    @pl.when(head)
    def _(): bias_copy.wait_send()
    @pl.when(jnp.logical_not(head))
    def _(): bias_copy.wait_recv()
    def step(k, _):
        for m in range(n):
            fam = head if not y_first[m] else True
            @pl.when(fam & (k <= z) & has_up)
            def _(): piece(m, 2 * k + x, up_sem, above).wait_send()
            @pl.when(fam & (k >= z) & has_down)
            def _(): piece(m, 2 * k + x, down_sem, below).wait_send()
            @pl.when(fam)
            def _(): piece(m, 2 * k + x, side_sem, side).wait_send()
            if not y_first[m]:
                @pl.when(head)
                def _():
                    piece(m, 2 * k, mate_sem, mate).wait_send()
                    piece(m, 2 * k + 1, mate_sem, mate).wait_send()
            else:
                @pl.when(head & (k == z))
                def _(): piece(m, quad, mate_sem, mate).wait_send()
        return 0
    lax.fori_loop(0, rows, step, 0)
    @pl.when(jnp.logical_not(head))
    def _():
        for m in range(n):
            pltpu.make_async_remote_copy(ins[m], outs[m].at[dp], own_send.at[m], own_recv.at[m], device_id=sibling, device_id_type=MESH).wait_send()

def gather(shards, bias, y_first, cid):
    count = chips()
    n = len(shards)
    dma = pltpu.SemaphoreType.DMA
    return pl.pallas_call(
        functools.partial(gather_kernel, count, y_first),
        out_shape=[jax.ShapeDtypeStruct((count,) + s.shape, s.dtype) for s in shards] + [jax.ShapeDtypeStruct(bias.shape, f32)],
        in_specs=[VMEM] * (n + 1),
        out_specs=[pl.BlockSpec(memory_space=pl.ANY)] * n + [VMEM],
        scratch_shapes=[dma((n, count // 2))] * 5 + [dma((n,))] * 3 + [dma((2,))],
        compiler_params=pltpu.CompilerParams(collective_id=cid, has_side_effects=True),
    )(*shards, bias)

def rcopy(src, dst, send, recv, dev):
    return pltpu.make_async_remote_copy(src, dst, send, recv, device_id=dev, device_id_type=MESH)

def ready(devs):
    bar = pltpu.get_barrier_semaphore()
    for dev, ok in devs:
        if ok is True:
            pl.semaphore_signal(bar, inc=1, device_id=dev, device_id_type=MESH)
        else:
            @pl.when(ok)
            def _(): pl.semaphore_signal(bar, inc=1, device_id=dev, device_id_type=MESH)
    return bar

def as_int(v): return v.astype(jnp.int32)

def halo_kernel(count, a_ref, win, sib_s, mate_s, far_s, recv, own_s):
    z, x, core, y = place()
    quad, quads = 2 * z + x, count // 2
    at_quad = lambda q: (q // 2, lax.rem(q, 2), core, y)
    sibling, mate = (z, x, 1 - core, y), (z, x, core, 1 - y)
    is1 = core == 1
    target, source = at_quad(quad - 1 + 2 * core), at_quad(quad + 1 - 2 * core)
    has_target = jnp.where(is1, quad + 1 < quads, quad > 0)
    has_source = jnp.where(is1, quad > 0, quad + 1 < quads)
    bar = ready([(sibling, True), (mate, True), (source, has_source)])
    own = 2 + 2 * core
    from_mate = 2 * core + 3 - 2 * y
    far = 6 - 6 * core
    passes = (core == y) & has_source
    extra = 5 - 4 * core
    takes = (core != y) & has_source
    @pl.when(quad == 0)
    def _():
        win[0] = jnp.zeros_like(win[0])
        @pl.when(y == 0)
        def _(): win[1] = jnp.zeros_like(win[1])
    @pl.when(quad == quads - 1)
    def _():
        win[6] = jnp.zeros_like(win[6])
        @pl.when(y == 1)
        def _(): win[5] = jnp.zeros_like(win[5])
    pl.semaphore_wait(bar, 2 + as_int(has_target))
    to_far = rcopy(a_ref, win.at[far], far_s.at[0], recv.at[far], target)
    to_mate = rcopy(a_ref, win.at[2 * core + 1 + 2 * y], mate_s.at[0], recv.at[2 * core + 1 + 2 * y], mate)
    to_sib = rcopy(a_ref, win.at[own], sib_s.at[own], recv.at[own], sibling)
    on = lambda w: rcopy(win.at[w], win.at[w], sib_s.at[w], recv.at[w], sibling)
    hand = rcopy(win.at[far], win.at[extra], mate_s.at[1], recv.at[extra], mate)
    @pl.when(has_target)
    def _(): to_far.start()
    to_mate.start()
    to_sib.start()
    win[own] = a_ref[...]
    on(from_mate).wait_recv()
    on(from_mate).start()
    @pl.when(has_source)
    def _():
        on(far).wait_recv()
        @pl.when(passes)
        def _(): hand.start()
        on(far).start()
    @pl.when(takes)
    def _():
        on(extra).wait_recv()
        on(extra).start()
    oc = 1 - core
    on(2 + 2 * oc).wait_recv()
    on(2 * oc + 3 - 2 * y).wait_recv()
    sib_source = jnp.where(is1, quad + 1 < quads, quad > 0)
    @pl.when(sib_source)
    def _():
        on(6 - 6 * oc).wait_recv()
    @pl.when(sib_source & (oc != y))
    def _(): on(5 - 4 * oc).wait_recv()
    @pl.when(has_target)
    def _(): to_far.wait_send()
    to_mate.wait_send()
    to_sib.wait_send()
    on(from_mate).wait_send()
    @pl.when(has_source)
    def _(): on(far).wait_send()
    @pl.when(passes)
    def _(): hand.wait_send()
    @pl.when(takes)
    def _(): on(extra).wait_send()

def halo(a, cid):
    count = chips()
    dma = pltpu.SemaphoreType.DMA
    return pl.pallas_call(
        functools.partial(halo_kernel, count),
        out_shape=jax.ShapeDtypeStruct((7,) + a.shape, a.dtype),
        in_specs=[VMEM], out_specs=VMEM,
        scratch_shapes=[dma((7,)), dma((2,)), dma((1,)), dma((7,)), dma((1,))],
        compiler_params=pltpu.CompilerParams(collective_id=cid, has_side_effects=True, vmem_limit_bytes=60 << 20),
    )(a)

def halo_back_kernel(count, p, out, sib_in, mate_in, far_in, stage, sib_s, sib_r, mate_s, mate_r, far_s, far_r):
    z, x, core, y = place()
    quad, quads = 2 * z + x, count // 2
    at_quad = lambda q: (q // 2, lax.rem(q, 2), core, y)
    sibling, mate = (z, x, 1 - core, y), (z, x, core, 1 - y)
    is1 = core == 1
    source, target = at_quad(quad - 1 + 2 * core), at_quad(quad + 1 - 2 * core)
    has_source = jnp.where(is1, quad + 1 < quads, quad > 0)
    has_target = jnp.where(is1, quad > 0, quad + 1 < quads)
    bar = ready([(sibling, True), (mate, True), (source, has_source)])
    pl.semaphore_wait(bar, 2 + as_int(has_target))
    own = 2 + 2 * core
    to_sib = lambda w: rcopy(p.at[w], sib_in.at[w], sib_s.at[w], sib_r.at[w], sibling)
    oc = 1 - core
    direct = lambda c: 2 * c + 3 - 2 * y
    far = lambda c: 6 - 6 * c
    extra = lambda c: 5 - 4 * c
    gives = (core != y) & has_target
    gets = (core == y) & has_target
    sib_has = has_source
    @pl.when(sib_has & (oc != y))
    def _(): to_sib(extra(oc)).start()
    to_sib(direct(oc)).start()
    @pl.when(sib_has)
    def _(): to_sib(far(oc)).start()
    to_sib(2 + 2 * oc).start()
    size = p.shape[1] // CUT
    at = lambda c: pl.ds(c * size, size)
    cuts = range(CUT)
    hand = lambda c: rcopy(stage.at[0, at(c)], mate_in.at[0, at(c)], mate_s.at[0, c], mate_r.at[0, c], mate)
    to_mate = lambda c: rcopy(stage.at[1, at(c)], mate_in.at[1, at(c)], mate_s.at[1, c], mate_r.at[1, c], mate)
    to_far = lambda c: rcopy(stage.at[2, at(c)], far_in.at[at(c)], far_s.at[c], far_r.at[c], target)
    both = lambda w, c: p[w, at(c)].astype(f32) + sib_in[w, at(c)].astype(f32)
    @pl.when(gives)
    def _():
        to_sib(extra(core)).wait_recv()
        for c in cuts:
            stage[0, at(c)] = both(extra(core), c).astype(bf16)
            hand(c).start()
    to_sib(direct(core)).wait_recv()
    for c in cuts:
        stage[1, at(c)] = both(direct(core), c).astype(bf16)
        to_mate(c).start()
    @pl.when(has_target)
    def _():
        to_sib(far(core)).wait_recv()
        @pl.when(gets)
        def _():
            for c in cuts:
                hand(c).wait_recv()
                stage[2, at(c)] = (both(far(core), c) + mate_in[0, at(c)].astype(f32)).astype(bf16)
                to_far(c).start()
        @pl.when(core != y)
        def _():
            for c in cuts:
                stage[2, at(c)] = both(far(core), c).astype(bf16)
                to_far(c).start()
    to_sib(own).wait_recv()
    for c in cuts:
        to_mate(c).wait_recv()
        out[at(c), :] = both(own, c) + mate_in[1, at(c)].astype(f32)
    @pl.when(has_source)
    def _():
        for c in cuts:
            to_far(c).wait_recv()
            out[at(c), :] = out[at(c), :] + far_in[at(c), :].astype(f32)
    @pl.when(sib_has & (oc != y))
    def _(): to_sib(extra(oc)).wait_send()
    to_sib(direct(oc)).wait_send()
    @pl.when(sib_has)
    def _(): to_sib(far(oc)).wait_send()
    to_sib(2 + 2 * oc).wait_send()
    @pl.when(gives)
    def _():
        for c in cuts: hand(c).wait_send()
    for c in cuts: to_mate(c).wait_send()
    @pl.when(has_target)
    def _():
        for c in cuts: to_far(c).wait_send()

CUT = 3

def halo_back(p, cid):
    count = chips()
    dma = pltpu.SemaphoreType.DMA
    one = p.shape[1:]
    return pl.pallas_call(
        functools.partial(halo_back_kernel, count),
        out_shape=jax.ShapeDtypeStruct(one, f32),
        in_specs=[VMEM], out_specs=VMEM,
        scratch_shapes=[pltpu.VMEM((7,) + one, bf16), pltpu.VMEM((2,) + one, bf16), pltpu.VMEM(one, bf16), pltpu.VMEM((3,) + one, bf16),
                        dma((7,)), dma((7,)), dma((2, CUT)), dma((2, CUT)), dma((CUT,)), dma((CUT,))],
        compiler_params=pltpu.CompilerParams(collective_id=cid, has_side_effects=True, vmem_limit_bytes=60 << 20),
    )(p)

def pair_gather_kernel(a_ref, out, send, recv):
    z, x, core, y = place()
    sibling = (z, x, 1 - core, y)
    pl.semaphore_wait(ready([(sibling, True)]), 1)
    copy = rcopy(a_ref, out.at[core], send, recv, sibling)
    copy.start()
    out[core] = a_ref[...]
    copy.wait()

def pair_gather(a, cid):
    return pl.pallas_call(
        pair_gather_kernel, out_shape=jax.ShapeDtypeStruct((2,) + a.shape, a.dtype), in_specs=[VMEM], out_specs=VMEM,
        scratch_shapes=[pltpu.SemaphoreType.DMA, pltpu.SemaphoreType.DMA],
        compiler_params=pltpu.CompilerParams(collective_id=cid, has_side_effects=True),
    )(a)

def pair_sum_kernel(p_ref, out, got, send, recv):
    z, x, core, y = place()
    sibling = (z, x, 1 - core, y)
    pl.semaphore_wait(ready([(sibling, True)]), 1)
    copy = rcopy(p_ref.at[1 - core], got, send, recv, sibling)
    copy.start()
    copy.wait()
    out[...] = p_ref[core].astype(f32) + got[...].astype(f32)

def pair_sum(p, cid):
    return pl.pallas_call(
        pair_sum_kernel, out_shape=jax.ShapeDtypeStruct(p.shape[1:], f32), in_specs=[VMEM], out_specs=VMEM,
        scratch_shapes=[pltpu.VMEM(p.shape[1:], p.dtype), pltpu.SemaphoreType.DMA, pltpu.SemaphoreType.DMA],
        compiler_params=pltpu.CompilerParams(collective_id=cid, has_side_effects=True),
    )(p)


def small_sum_kernel(rows, layers, *refs):
    per = 9
    ins, refs = refs[:layers * per], refs[layers * per:]
    gains, shifts, obias, qvb, upb, v, got, acc, zin, send, recv, z_s, z_r = refs
    z, x, core, y = place()
    width, half = v.shape[1], v.shape[1] // 2
    spans_up = ins[per - 1].shape[0] // width
    stride = 8 + 2 * spans_up
    peers = [(z, x, 1 - core, y), (z, 1 - x, core, y), (z, x, core, 1 - y)]
    others = [lax.rem(z + d, rows) for d in range(1, rows)]
    at = lambda o: (o, x, core, y)
    bar = ready([(p, True) for p in peers] + [(at(o), True) for o in others])
    v[...] = jnp.zeros_like(v)
    for l in range(layers):
        one, b = ins[l * per:(l + 1) * per], l * stride
        for i in range(6): v[b + i, :] = one[i][...]
        for c in range(2):
            @pl.when(core == c)
            def _():
                for i in range(2): v[b + 6 + i:b + 7 + i, c * half:(c + 1) * half] = one[6 + i][...]
                for i in range(spans_up):
                    r = b + 8 + c * spans_up + i
                    v[r, :] = one[8][i * width:(i + 1) * width]
    pl.semaphore_wait(bar, 3 + rows - 1)
    src = v
    for i, p in enumerate(peers):
        copy = rcopy(src, got.at[i], send.at[i], recv.at[i], p)
        copy.start()
        copy.wait()
        acc[i] = src[...] + got[i]
        src = acc.at[i]
    to = lambda o, slot: rcopy(src, zin.at[slot], z_s.at[o], z_r.at[slot], at(o))
    for o in others: to(o, z).start()
    zin[z] = src[...]
    for o in others: to(o, o).wait_recv()
    total = zin[0]
    for i in range(1, rows): total = total + zin[i]
    v[...] = total
    for l in range(layers):
        b = l * stride
        for i in range(2):
            gains[l, i:i + 1, :] = v[b + i:b + i + 1, :]
            shifts[l, i:i + 1, :] = v[b + 2 + i:b + 3 + i, :]
            obias[l, i:i + 1, :] = v[b + 4 + i:b + 5 + i, :]
        for c in range(2):
            @pl.when(y == c)
            def _():
                for i in range(2): qvb[l, i:i + 1, :] = v[b + 6 + i:b + 7 + i, c * half:(c + 1) * half]
                for i in range(spans_up):
                    r = b + 8 + c * spans_up + i
                    upb[l:l + 1, i * width:(i + 1) * width] = v[r:r + 1, :]
    for o in others: to(o, z).wait_send()

def small_sum(parts, cid):
    rows = lax.axis_size("z")
    dma = pltpu.SemaphoreType.DMA
    layers, width, hidden = len(parts), parts[0][0].shape[0], parts[0][8].shape[0]
    flat = [t for p in parts for t in p]
    one = (layers * (8 + 2 * hidden // width), width)
    pair = jax.ShapeDtypeStruct((layers, 2, width), f32)
    return pl.pallas_call(
        functools.partial(small_sum_kernel, rows, layers),
        out_shape=[pair, pair, pair, jax.ShapeDtypeStruct((layers, 2, width // 2), f32), jax.ShapeDtypeStruct((layers, hidden), f32)],
        in_specs=[VMEM] * len(flat), out_specs=[VMEM] * 5,
        scratch_shapes=[pltpu.VMEM(one, f32), pltpu.VMEM((3,) + one, f32), pltpu.VMEM((3,) + one, f32), pltpu.VMEM((rows,) + one, f32),
                        dma((3,)), dma((3,)), dma((rows,)), dma((rows,))],
        compiler_params=pltpu.CompilerParams(collective_id=cid, has_side_effects=True, vmem_limit_bytes=60 << 20),
    )(*flat)

def reduce_kernel(count, early, *refs):
    n = len(early)
    rows = count // 4
    grads, outs = refs[:n], refs[n:2*n]
    k = 2*n
    mate_in, side_out, side_in, line_out, up_in, down_in, final_out = [refs[k+i*n:k+(i+1)*n] for i in range(7)]
    k += 7*n
    (mate_s, mate_r, side_s, side_r, up_s, up_r, down_s, down_r, last_s, last_r) = refs[k:]
    z, x, core, y = place()
    quad = 2 * z + x
    dp = 2 * quad + core
    head = core == y
    other = jnp.logical_not(head)
    sibling = (z, x, 1 - core, y)
    side = (z, 1 - x, core, y)
    above = (z + 1, x, core, y)
    below = (z - 1, x, core, y)
    mate = (z, x, core, 1 - y)
    has_up = z + 1 < rows
    has_down = z > 0
    for m in range(n):
        @pl.when(z == 0)
        def _(): up_in[m][...] = jnp.zeros_like(up_in[m])
        @pl.when(z == rows - 1)
        def _(): down_in[m][...] = jnp.zeros_like(down_in[m])
    bar = pltpu.get_barrier_semaphore()
    def sig(dev): pl.semaphore_signal(bar, inc=1, device_id=dev, device_id_type=MESH)
    sig(side)
    @pl.when(has_up)
    def _(): sig(above)
    @pl.when(has_down)
    def _(): sig(below)
    @pl.when(head)
    def _(): sig(mate)
    @pl.when(other)
    def _(): sig(sibling)
    pl.semaphore_wait(bar, 2 + has_up.astype(jnp.int32) + has_down.astype(jnp.int32))

    def rc(src, dst, s, r, dev):
        return pltpu.make_async_remote_copy(src, dst, s, r, device_id=dev, device_id_type=MESH)
    def to_mate(m, q):
        return rc(grads[m].at[pl.ds(2*q, 2)], mate_in[m].at[pl.ds(2*q, 2)], mate_s.at[m, q], mate_r.at[m, q], mate)
    def to_side(m, j):
        return rc(side_out[m].at[j], side_in[m].at[j], side_s.at[m, j], side_r.at[m, j], side)
    def to_up(m, j):
        return rc(line_out[m].at[j], up_in[m].at[j], up_s.at[m, j], up_r.at[m, j], above)
    def to_down(m, j):
        return rc(line_out[m].at[j], down_in[m].at[j], down_s.at[m, j], down_r.at[m, j], below)
    def late_mate(m):
        return rc(line_out[m].at[z], mate_in[m], mate_s.at[m, quad], mate_r.at[m, quad], mate)
    def last(m):
        return rc(final_out[m], outs[m], last_s.at[m], last_r.at[m], sibling)

    def far_first(fn):
        def step(i, _):
            d = rows - i
            for j, ok in ((z + d, z + d < rows), (z - d, z - d >= 0)):
                @pl.when(ok)
                def _(): fn(j)
            return 0
        lax.fori_loop(1, rows, step, 0)
        fn(z)

    order = [m for m in range(n) if early[m]], [m for m in range(n) if not early[m]]

    @pl.when(other)
    def _():
        def go(j):
            for m in order[0]:
                to_mate(m, 2 * j + 1 - x).start()
        def go2(j):
            for m in order[0]:
                to_mate(m, 2 * j + x).start()
        far_first(go); far_first(go2)

    def own(m, q, c, with_mate):
        t = grads[m][2*q+c].astype(f32)
        return t + mate_in[m][2*q+c].astype(f32) if with_mate else t

    def side_stage(ms, with_mate):
        def go(j):
            q = 2 * j + 1 - x
            for m in ms:
                if with_mate: to_mate(m, q).wait_recv()
                def half(c, _):
                    side_out[m][j, c] = own(m, q, c, with_mate).astype(bf16)
                    return 0
                lax.fori_loop(0, 2, half, 0)
            for m in ms:
                to_side(m, j).start()
        far_first(go)

    def line_stage(ms, with_mate):
        def go(j):
            q = 2 * j + x
            for m in ms:
                if with_mate: to_mate(m, q).wait_recv()
                to_side(m, j).wait_recv()
                @pl.when((j >= z) & has_down)
                def _(): to_up(m, j).wait_recv()
                @pl.when((j <= z) & has_up)
                def _(): to_down(m, j).wait_recv()
                def half(c, _):
                    t = own(m, q, c, with_mate) + side_in[m][j, c].astype(f32)
                    @pl.when(j > z)
                    def _(): line_out[m][j, c] = (t + up_in[m][j, c].astype(f32)).astype(bf16)
                    @pl.when(j < z)
                    def _(): line_out[m][j, c] = (t + down_in[m][j, c].astype(f32)).astype(bf16)
                    @pl.when(j == z)
                    def _():
                        u = t + up_in[m][j, c].astype(f32) + down_in[m][j, c].astype(f32)
                        if with_mate:
                            @pl.when(c == core)
                            def _(): outs[m][...] = u
                            @pl.when(c != core)
                            def _(): final_out[m][...] = u
                        else:
                            @pl.when(other)
                            def _(): line_out[m][j, c] = u.astype(bf16)
                            @pl.when(head & (c == core))
                            def _(): outs[m][...] = u
                            @pl.when(head & (c != core))
                            def _(): final_out[m][...] = u
                    return 0
                lax.fori_loop(0, 2, half, 0)
            for m in ms:
                @pl.when(j > z)
                def _(): to_up(m, j).start()
                @pl.when(j < z)
                def _(): to_down(m, j).start()
        far_first(go)

    side_stage(order[1], False)
    @pl.when(head)
    def _(): side_stage(order[0], True)
    line_stage(order[1], False)
    @pl.when(other)
    def _():
        for m in order[1]: late_mate(m).start()
    @pl.when(head)
    def _():
        line_stage(order[0], True)
        for m in order[1]:
            late_mate(m).wait_recv()
            outs[m][...] = outs[m][...] + mate_in[m][core].astype(f32)
            final_out[m][...] = final_out[m][...] + mate_in[m][1 - core].astype(f32)
        for m in range(n):
            last(m).start()
    @pl.when(other)
    def _():
        for m in range(n): last(m).wait_recv()
    def step(j, _):
        for m in range(n):
            fam = head if early[m] else True
            @pl.when(fam)
            def _(): to_side(m, j).wait_send()
            @pl.when(fam & (j > z))
            def _(): to_up(m, j).wait_send()
            @pl.when(fam & (j < z))
            def _(): to_down(m, j).wait_send()
            if early[m]:
                @pl.when(other)
                def _():
                    to_mate(m, 2 * j).wait_send()
                    to_mate(m, 2 * j + 1).wait_send()
        return 0
    lax.fori_loop(0, rows, step, 0)
    for m in range(n):
        @pl.when(head)
        def _(): last(m).wait_send()
        if not early[m]:
            @pl.when(other)
            def _(): late_mate(m).wait_send()

def scatter_sum(grads, early, cid):
    count = chips()
    n = len(grads)
    rows = count // 4
    dma = pltpu.SemaphoreType.DMA
    quads = [pltpu.VMEM((rows, 2) + g.shape[1:], bf16) for g in grads]
    mates = [pltpu.VMEM(((count if e else 2),) + g.shape[1:], bf16) for g, e in zip(grads, early)]
    lasts = [pltpu.VMEM(g.shape[1:], f32) for g in grads]
    return pl.pallas_call(
        functools.partial(reduce_kernel, count, early),
        out_shape=[jax.ShapeDtypeStruct(g.shape[1:], f32) for g in grads],
        in_specs=[pl.BlockSpec(memory_space=pltpu.VMEM)] * n,
        out_specs=[pl.BlockSpec(memory_space=pltpu.VMEM)] * n,
        scratch_shapes=mates + quads * 5 + lasts + [dma((n, count // 2))] * 2 + [dma((n, rows))] * 6 + [dma((n,))] * 2,
        compiler_params=pltpu.CompilerParams(collective_id=cid, has_side_effects=True, vmem_limit_bytes=60 << 20),
    )(*grads)
TQ, TK, BQ, BK = 384, 512, 384, 512
NEG = -1e30

def nt(a, b):
    return lax.dot_general(a, b, (((1,), (1,)), ((), ())), preferred_element_type=f32)
def tn(a, b):
    return lax.dot_general(a, b, (((0,), (0,)), ((), ())), preferred_element_type=f32)

def fold(t, op):
    out = t[:, :128]
    for i in range(1, t.shape[1] // 128):
        out = op(out, t[:, i*128:(i+1)*128])
    return out

def tiled(t, n):
    return t if n == 128 else jnp.concatenate([t] * (n // 128), axis=1)

def tile_at(lo, j, size, wide):
    want = lo + j * size
    start = jnp.minimum(want, wide - size)
    return pl.multiple_of(start, 128), want - start

def fwd_kernel(half, span_ref, q_ref, k_ref, v_ref, idq_ref, idk_ref, o_ref, lse_ref, s_scr, m_scr, l_scr, acc):
    i = pl.program_id(0)
    T = q_ref.shape[0]
    pairs = q_ref.shape[1] // 128
    wide = k_ref.shape[0]
    lo, steps = span_ref[0, i], span_ref[1, i]
    low = lax.broadcasted_iota(jnp.int32, (T, 128), 1) < 64
    qs = []
    for p in range(pairs):
        qp = q_ref[:, p*128:(p+1)*128] * jnp.bfloat16(0.125)
        z = jnp.zeros_like(qp)
        qs += [jnp.where(low, qp, z), jnp.where(low, z, qp)]
    gap = 2 * half + i * T + jnp.where(i >= half // T, half, 0)
    idq = idq_ref[...]
    col = lax.broadcasted_iota(jnp.int32, (T, TK), 1)
    rel = col - lax.broadcasted_iota(jnp.int32, (T, TK), 0)
    for h in range(2 * pairs):
        m_scr[h] = jnp.full((T, 128), NEG, f32)
        l_scr[h] = jnp.zeros((T, 128), f32)
    for p in range(pairs):
        acc[p] = jnp.zeros((T, 128), f32)
    def scores(j, _):
        start, fresh = tile_at(lo, j, TK, wide)
        ok = ((idq == idk_ref[0:1, pl.ds(start, TK)]) | (rel == gap - start)) & (col >= fresh)
        for h in range(2 * pairs):
            p = h // 2
            s = jnp.where(ok, nt(qs[h], k_ref[pl.ds(start, TK), p*128:(p+1)*128]), NEG)
            s_scr[h, j] = s
            m_scr[h] = jnp.maximum(m_scr[h], fold(s, jnp.maximum))
        return 0
    lax.fori_loop(0, steps, scores, 0)
    for h in range(2 * pairs):
        m_scr[h] = jnp.broadcast_to(jnp.max(m_scr[h], axis=1, keepdims=True), (T, 128))
    def values(j, _):
        start, fresh = tile_at(lo, j, TK, wide)
        for p in range(pairs):
            vp = v_ref[pl.ds(start, TK), p*128:(p+1)*128]
            out = []
            for h in (2*p, 2*p+1):
                e = jnp.exp(s_scr[h, j] - tiled(m_scr[h], TK))
                l_scr[h] = l_scr[h] + fold(e, jnp.add)
                out.append(jnp.dot(e.astype(bf16), vp, preferred_element_type=f32))
            acc[p] = acc[p] + jnp.where(low, out[0], out[1])
        return 0
    lax.fori_loop(0, steps, values, 0)
    for p in range(pairs):
        inv = [1.0 / jnp.sum(l_scr[h], axis=1, keepdims=True) for h in (2*p, 2*p+1)]
        o_ref[:, p*128:(p+1)*128] = (acc[p] * jnp.where(low, inv[0], inv[1])).astype(bf16)
    for h in range(2 * pairs):
        total = jnp.sum(l_scr[h].T, axis=0, keepdims=True)
        lse_ref[h:h+1, :] = m_scr[h].T[0:1, :] + jnp.log(total)

def attend(q, k, v, span, idq, idk):
    rows, cols = q.shape
    wide = k.shape[0]
    heads = cols // 64
    tiles = rows // TQ
    full = lambda a: pl.BlockSpec(a.shape, lambda i, s: (0,) * a.ndim)
    most = (4 * (rows // 2) + TQ + TK) // TK + 1
    return pl.pallas_call(
        functools.partial(fwd_kernel, rows // 2),
        grid_spec=pltpu.PrefetchScalarGridSpec(
            num_scalar_prefetch=1, grid=(tiles,),
            in_specs=[pl.BlockSpec((TQ, cols), lambda i, s: (i, 0)), full(k), full(v),
                      pl.BlockSpec((TQ, 1), lambda i, s: (i, 0)), full(idk)],
            out_specs=[pl.BlockSpec((TQ, cols), lambda i, s: (i, 0)), pl.BlockSpec((heads, TQ), lambda i, s: (0, i))],
            scratch_shapes=[pltpu.VMEM((heads, most, TQ, TK), f32), pltpu.VMEM((heads, TQ, 128), f32), pltpu.VMEM((heads, TQ, 128), f32),
                            pltpu.VMEM((heads // 2, TQ, 128), f32)]),
        out_shape=[jax.ShapeDtypeStruct((rows, cols), bf16), jax.ShapeDtypeStruct((heads, rows), f32)],
        compiler_params=pltpu.CompilerParams(vmem_limit_bytes=60 << 20, dimension_semantics=("arbitrary",)),
        cost_estimate=pl.CostEstimate(flops=4*rows*wide*cols, bytes_accessed=6*wide*cols, transcendentals=0),
    )(span, q, k, v, idq, idk)

def bwd_kernel(half, span_ref, q_ref, k_ref, v_ref, o_ref, da_ref, lse_ref, idq_ref, idk_ref, d_ref, qb_ref, vb_ref, dk_acc, dv_acc, dq_acc):
    i = pl.program_id(0)
    T = q_ref.shape[0]
    pairs = q_ref.shape[1] // 128
    wide, cols = k_ref.shape
    lo, steps = span_ref[0, i], span_ref[1, i]
    low = lax.broadcasted_iota(jnp.int32, (T, 128), 1) < 64
    @pl.when(i == 0)
    def _():
        dk_acc[...] = jnp.zeros_like(dk_acc)
        dv_acc[...] = jnp.zeros_like(dv_acc)
        d_ref[:, :cols] = jnp.zeros((wide, cols), bf16)
        qb_ref[...] = jnp.zeros_like(qb_ref)
    qs, das, delta = [], [], []
    for p in range(pairs):
        at = slice(p*128, (p+1)*128)
        qp = q_ref[:, at] * jnp.bfloat16(0.125)
        dp = da_ref[:, at]
        z = jnp.zeros_like(qp)
        qs += [jnp.where(low, qp, z), jnp.where(low, z, qp)]
        das += [jnp.where(low, dp, z), jnp.where(low, z, dp)]
        t = (dp.astype(f32) * o_ref[:, at].astype(f32)).T
        delta += [jnp.sum(t[:64], axis=0, keepdims=True), jnp.sum(t[64:], axis=0, keepdims=True)]
        dq_acc[p] = jnp.zeros((T, 128), f32)
    gap = 2 * half + i * T + jnp.where(i >= half // T, half, 0)
    idq = idq_ref[...]
    row = lax.broadcasted_iota(jnp.int32, (BK, T), 0)
    rel = row - lax.broadcasted_iota(jnp.int32, (BK, T), 1)
    def tile(j, _):
        start, fresh = tile_at(lo, j, BK, wide)
        at_rows = pl.ds(start, BK)
        ok = ((idk_ref[at_rows, :] == idq) | (rel == gap - start)) & (row >= fresh)
        for p in range(pairs):
            at = slice(p*128, (p+1)*128)
            kp, vp = k_ref[at_rows, at], v_ref[at_rows, at]
            kx = kp * jnp.bfloat16(0.125)
            dk = dv = 0
            dq = []
            for h in (2*p, 2*p+1):
                s = jnp.where(ok, nt(kp, qs[h]), NEG)
                pr = jnp.exp(s - lse_ref[h:h+1, :])
                ds = (pr * (nt(vp, das[h]) - delta[h])).astype(bf16)
                dv = dv + jnp.dot(pr.astype(bf16), das[h], preferred_element_type=f32)
                dk = dk + jnp.dot(ds, qs[h], preferred_element_type=f32)
                dq.append(tn(ds, kx))
            dq_acc[p] = dq_acc[p] + jnp.where(low, dq[0], dq[1])
            dk_acc[at_rows, at] = dk_acc[at_rows, at] + dk
            dv_acc[at_rows, at] = dv_acc[at_rows, at] + dv
        return 0
    lax.fori_loop(0, steps, tile, 0)
    for p in range(pairs):
        at = slice(p*128, (p+1)*128)
        d_ref[pl.ds(pl.multiple_of(gap, 128), T), at] = dq_acc[p].astype(bf16)
        qb_ref[:, at] = qb_ref[:, at] + jnp.sum(dq_acc[p], axis=0, keepdims=True)
    @pl.when(i == pl.num_programs(0) - 1)
    def _():
        d_ref[:, cols:2*cols] = dk_acc[...].astype(bf16)
        d_ref[:, 2*cols:] = dv_acc[...].astype(bf16)
        vb_ref[...] = jnp.sum(dv_acc[...], axis=0, keepdims=True)

def attend_back(q, k, v, o, da, lse, span, idq_row, idk_col):
    rows, cols = q.shape
    wide = k.shape[0]
    heads = cols // 64
    tiles = rows // BQ
    full = lambda a: pl.BlockSpec(a.shape, lambda i, s: (0,) * a.ndim)
    qt = pl.BlockSpec((BQ, cols), lambda i, s: (i, 0))
    return pl.pallas_call(
        functools.partial(bwd_kernel, rows // 2),
        grid_spec=pltpu.PrefetchScalarGridSpec(
            num_scalar_prefetch=1, grid=(tiles,),
            in_specs=[qt, full(k), full(v), qt, qt, pl.BlockSpec((heads, BQ), lambda i, s: (0, i)),
                      pl.BlockSpec((1, BQ), lambda i, s: (0, i)), full(idk_col)],
            out_specs=[pl.BlockSpec((wide, 3 * cols), lambda i, s: (0, 0))] + [pl.BlockSpec((1, cols), lambda i, s: (0, 0))] * 2,
            scratch_shapes=[pltpu.VMEM((wide, cols), f32), pltpu.VMEM((wide, cols), f32), pltpu.VMEM((heads // 2, BQ, 128), f32)]),
        out_shape=[jax.ShapeDtypeStruct((wide, 3 * cols), bf16)] + [jax.ShapeDtypeStruct((1, cols), f32)] * 2,
        compiler_params=pltpu.CompilerParams(vmem_limit_bytes=60 << 20, dimension_semantics=("arbitrary",)),
        cost_estimate=pl.CostEstimate(flops=10*rows*wide*cols, bytes_accessed=10*wide*cols, transcendentals=0),
    )(span, q, k, v, o, da, lse, idq_row, idk_col)

def spans(ids, mine, tq, tk):
    first, final = mine[::tq], mine[tq-1::tq]
    lo = jnp.sum((ids[None, :] < first[:, None]).astype(jnp.int32), axis=1) // 128 * 128
    hi = jnp.sum((ids[None, :] <= final[:, None]).astype(jnp.int32), axis=1)
    return jnp.stack([lo, (hi - lo + tk - 1) // tk])

def window_ids(clip_ids, frame_mask, half):
    z, x, core, y = place()
    start = (4 * (2 * z + x) + y) * half
    pad = 4 * half
    ids = jnp.pad(clip_ids, (2 * half, pad), constant_values=((-1, 1 << 30),))
    val = jnp.pad(frame_mask, (2 * half, pad))
    ids = lax.dynamic_slice_in_dim(ids, start, 7 * half)
    val = lax.dynamic_slice_in_dim(val, start, 7 * half)
    mine = jnp.concatenate([ids[2*half:3*half], ids[4*half:5*half]])
    keys = jnp.where(val == 1, ids, -2)
    return spans(ids, mine, TQ, TK), spans(ids, mine, BQ, BK), mine, keys

def norm_forward(values, gain_vec, bias_vec):
    row_mean = jnp.mean(values, axis=-1, keepdims=True)
    centred = values - row_mean
    inverse = lax.rsqrt(jnp.mean(centred * centred, axis=-1, keepdims=True) + EPS)
    normed = centred * inverse
    return ((normed * gain_vec + bias_vec).astype(bf16), normed, inverse)

def norm_backward(grad_out, normed, inverse, gain_vec):
    scaled = grad_out * gain_vec
    projected = (scaled - jnp.mean(scaled, axis=-1, keepdims=True)
                 - normed * jnp.mean(scaled * normed, axis=-1, keepdims=True))
    return (inverse * projected, jnp.sum(grad_out * normed, axis=0), jnp.sum(grad_out, axis=0))

def gelu_parts(z):
    half = 0.5 * (1.0 + jax.scipy.special.erf(z * 0.7071067811865476))
    return z * half, half + z * jnp.exp(-0.5 * z * z) * 0.3989422804014327

def mm(a, b):
    return jnp.dot(a, b, preferred_element_type=f32)

def pack(parts, width):
    return jnp.concatenate([p[..., i:i + width] for p in parts for i in range(0, p.shape[-1], width)], axis=1)

def unpack(packed, shapes, width):
    out, at = [], 0
    for r, c in shapes:
        n = c // width
        out.append(jnp.concatenate([packed[:, at + i * r:at + (i + 1) * r] for i in range(n)], axis=-1))
        at += n * r
    return out

def swap(t):
    return lax.ppermute(t, ("core", "y"), [(0, 0), (1, 2), (2, 1), (3, 3)])

def body(frames_in, frames_cot, clip_ids, frame_mask, norm_gain, norm_bias, qkv_weight, qv_bias,
         proj_weight, up_weight, up_bias, down_weight, out_biases):
    layers = qkv_weight.shape[0]
    half, width = frames_in.shape
    z, x, core, y = place()
    count = chips()
    group = ("z", "x", "y")
    hcols = qkv_weight.shape[-1]
    hidden = up_weight.shape[-1]
    span, span_back, mine, keys = window_ids(clip_ids, frame_mask, half)
    idk = keys[None, :]
    shards = [[qkv_weight[l].reshape(-1, 3 * hcols), proj_weight[l], up_weight[l], down_weight[l]] for l in range(layers)]
    bias = jnp.concatenate([up_bias, qv_bias.reshape(layers, 2 * hcols)], axis=1)
    halves = lambda t: t.reshape(-1, width)
    soon = [shards[0][3], halves(shards[1][0])]
    late = shards[1][2:]
    moved = swap(pack([t[None] for t in soon], width)[0])
    moved_late = swap(pack([t[None] for t in late], width)[0])
    wqkv0, wproj0, wup0, wproj1, bias = gather(shards[0][:3] + shards[1][1:2], bias, [False, True, True, False], 0)
    moved, wqkv0, wproj0, wup0 = lax.optimization_barrier((moved, wqkv0, wproj0, wup0))
    every = lambda t: lax.all_gather(t, group, axis=0, tiled=False)
    rows_of = lambda w: w.reshape(-1, w.shape[-1])
    got = every(moved)
    full = [[rows_of(wqkv0), rows_of(wproj0), rows_of(wup0), None], None]
    state = frames_in
    kept = []
    for l in range(layers):
        wqkv = full[l][0]
        upb, qb, vb = bias[l, :hidden], bias[l, hidden:hidden+hcols], bias[l, hidden+hcols:]
        a, hat1, inv1 = norm_forward(state, norm_gain[l, 0], norm_bias[l, 0])
        win = halo(a, 1)
        a_own = jnp.concatenate([win[2], win[4]])
        a_win = win.reshape(-1, width)
        q = (mm(a_own, wqkv[:, :hcols]) + qb).astype(bf16)
        k = mm(a_win, wqkv[:, hcols:2*hcols]).astype(bf16)
        v = (mm(a_win, wqkv[:, 2*hcols:]) + vb).astype(bf16)
        o, lse = attend(q, k, v, span, mine[:, None], idk)
        if l > 0:
            o, got = lax.optimization_barrier((o, got))
            full[1] += [rows_of(wproj1)] + [rows_of(w) for w in unpack(got, [t.shape for t in late], width)]
        wqkv, wproj, wup, wdown = full[l]
        middle = state + pair_sum(mm(o, wproj).astype(bf16).reshape(2, half, width), 2) + out_biases[l, 0]
        c, hat2, inv2 = norm_forward(middle, norm_gain[l, 1], norm_bias[l, 1])
        c_full = pair_gather(c, 3).reshape(2 * half, width)
        zz = mm(c_full, wup) + upb
        g, slope = gelu_parts(zz)
        g, slope = g.astype(bf16), slope.astype(bf16)
        if l == 0:
            g, got = lax.optimization_barrier((g, got))
            wdown, nxt = [rows_of(w) for w in unpack(got, [t.shape for t in soon], width)]
            moved_late, wdown = lax.optimization_barrier((moved_late, wdown))
            full[0][3] = wdown
            full[1] = [nxt.reshape(-1, 3 * hcols)]
            got = every(moved_late)
        state = middle + pair_sum(mm(g, wdown).astype(bf16).reshape(2, half, width), 2) + out_biases[l, 1]
        kept.append((a_own, a_win, hat1, inv1, q, k, v, o, lse, hat2, inv2, c_full, g, slope))
    grad = frames_cot
    wgrads, small = [None] * layers, [None] * layers
    for l in reversed(range(layers)):
        wqkv, wproj, wup, wdown = full[l]
        a_own, a_win, hat1, inv1, q, k, v, o, lse, hat2, inv2, c_full, g, slope = kept[l]
        e_full = pair_gather(grad.astype(bf16), 3).reshape(2 * half, width)
        g_down = mm(g.T, e_full)
        dz = mm(e_full, wdown.T) * slope.astype(f32)
        upb = jnp.sum(dz, axis=0)
        dzb = dz.astype(bf16)
        g_up = mm(c_full.T, dzb)
        dc = pair_sum(mm(dzb, wup.T).astype(bf16).reshape(2, half, width), 2)
        back, gain2, shift2 = norm_backward(dc, hat2, inv2, norm_gain[l, 1])
        dh = grad + back
        dh_full = pair_gather(dh.astype(bf16), 3).reshape(2 * half, width)
        g_proj = mm(o.T, dh_full)
        da = mm(dh_full, wproj.T).astype(bf16)
        dqkv, qb, vb = attend_back(q, k, v, o, da, lse, span_back, mine[None, :], keys[:, None])
        g_qkv = mm(a_win.T, dqkv)
        part = mm(dqkv, wqkv.T).astype(bf16).reshape(7, half, width)
        da1 = halo_back(part, 4)
        back, gain1, shift1 = norm_backward(da1, hat1, inv1, norm_gain[l, 0])
        small[l] = [gain1, gain2, shift1, shift2, jnp.sum(dh, axis=0), jnp.sum(grad, axis=0), qb, vb, upb]
        grad = dh + back
        grads = [t.astype(bf16).reshape(count, -1, t.shape[-1]) for t in (g_qkv, g_proj, g_up, g_down)]
        if l == 0:
            wgrads[l] = scatter_sum(grads, [False, True, False, True], 5)
        else:
            packed = pack(grads, hcols)
            packed, grad = lax.optimization_barrier((packed, grad))
            rows = packed.shape[1]
            own = lax.psum_scatter(packed.reshape(-1, hcols), group, scatter_dimension=0, tiled=True)
    wgrads[0] = list(wgrads[0])
    own, wgrads[0][1] = lax.optimization_barrier((own, wgrads[0][1]))
    wgrads[1] = [w[0] for w in unpack(swap(own)[None].astype(f32), [s.shape for s in shards[1]], hcols)]
    wgrads[0][0], small[0][0] = lax.optimization_barrier((wgrads[0][0], small[0][0]))
    gains, shifts, obias, qvb, upb = small_sum(small, 6)
    gq, gp, gu, gd = [jnp.stack([w[i] for w in wgrads]) for i in range(4)]
    return (state, grad, gq.reshape(layers, -1, 3, hcols), qvb, gp, gu, upb, gd, gains, shifts, obias)

def solution(mesh):
    dp, mp = mesh.shape["dp"], mesh.shape["mp"]
    named = Mesh(mesh.devices.reshape(dp // 4, 2, 2, mp), ("z", "x", "core", "y"))
    deep = ("z", "x", "core")
    rows = P(deep + ("y",), None)
    qkv, qv = P(None, deep, None, "y"), P(None, None, "y")
    tall, wide, upb = P(None, ("y",) + deep, None), P(None, deep, "y"), P(None, "y")
    return jax.shard_map(
        body, mesh=named,
        in_specs=(rows, rows, P(), P(), P(), P(), qkv, qv, tall, wide, upb, tall, P()),
        out_specs=(rows, rows, qkv, qv, tall, wide, upb, tall, P(), P(), P()),
        check_vma=False)
```
